256 devices in a mesh: dp: 32 (over y, x, core), ka: 8 (over z).
Axes of the slice: x: 4, y: 4, z: 8, core: 2. Of those that a mesh axis runs over, the one named last changes fastest.
Arguments:
- feats: bfloat16 [65536, 256], P('dp'), may hold values from -6 to 6
- coords: float32 [3, 65536], P(None, 'dp'), may hold values from 0 to 1
- cell_ids: int32 [32, 2048], P('dp'), may hold values from 0 to 7, never falling along the last dimension, each value on 1 to 1024 neighbouring positions
- recip: float32 [32, 8, 9], P('dp'), may hold values from 0.05 to 0.35
- kvec: int32 [3, 1024], P(None, 'ka'), may hold values from -4 to 4
- w_in: bfloat16 [256, 256], replicated, may hold values from -0.375 to 0.375
- w_out: bfloat16 [256, 256], replicated, may hold values from -0.375 to 0.375
- kfilt: float32 [1024, 256], P('ka'), may hold values from -3 to 3
- spread: float32 [256], replicated, may hold values from 0.02 to 0.5
- cotan: bfloat16 [65536, 256], P('dp'), may hold values from -6 to 6
Outputs:
- mixed: bfloat16 [65536, 256], P('dp')
- feat_grad: bfloat16 [65536, 256], P('dp')
- grad_w_in: float32 [256, 256], replicated
- grad_w_out: float32 [256, 256], replicated
- grad_kfilt: float32 [1024, 256], P('ka')
The draws below stay inside these ranges and needn't reach their ends.
Inputs may be any that keep to these rules, and one draw needn't show every extreme that they name: `cell_ids`: within each row, cell numbers never fall; each of the 8 cells holds 1 to 1024 atoms, and one holds exactly 1024.
All inputs are finite; a program needn't handle non-finite values.
Results may differ from the reference program's by a relative error of at most 0.0056.
The reference program's roundings to bfloat16 on the way (of `projected`, `activated`, `message_grad` and `update`) count: a program that leaves them out, or rounds other values in their place, can miss the bound.
Values may be sent and summed in bfloat16 or wider, within the bound.
A program may use at most 64 MiB of HBM per device.

```python
import math
import jax
import jax.numpy as jnp
import numpy as np
from jax import lax

C = 256
ATOM_DEV = 2048
CELL_DEV = 8
MOST = 1024
K = 1024
ATOMS = 65536
N_DP = 32


def touch_ends(array, rng, low, largest):
    dims = array.shape
    spot = [jax.random.randint(jax.random.fold_in(rng, axis), (), 0, dims[axis]) for axis in range(len(dims))]
    array = array.at[tuple(spot)].set(low)
    longest = dims.index(max(dims))
    spot[longest] = (spot[longest] + 1) % dims[longest]
    return array.at[tuple(spot)].set(largest)


def level_of(key, dims, pieces, least, top_value):
    loudness = 1.0
    for position, shards_of in pieces:
        steps = jax.random.uniform(jax.random.fold_in(jax.random.fold_in(key, 6), position), (shards_of,), jnp.float32, least / len(pieces), top_value / len(pieces))
        loudness = loudness * jnp.repeat(jnp.exp(steps), dims[position] // shards_of).reshape((-1,) + (1,) * (len(dims) - 1 - position))
    return loudness


def split_up(amount, total, bound, slope):
    weights = [(1 << 20) // math.isqrt(standing ** slope) + 1 for standing in range(2, amount + 1)]
    spare, given = total - bound - (amount - 1), [1] * (amount - 1)
    while spare > 0:
        free = [i for i in range(amount - 1) if given[i] < bound]
        pool, budget = sum([weights[i] for i in free]), spare
        for i in free:
            more = min(bound - given[i], max(1, budget * weights[i] // pool), spare)
            given[i] = given[i] + more
            spare = spare - more
    return np.array([bound] + given)


def uneven_parts(rng, number_of, total, most, slope):
    if number_of == 2:
        one = jax.random.randint(rng, (), max(1, total - most), min(most, total - 1) + 1)
        return jnp.stack([one, total - one])
    sizes = jnp.asarray(split_up(number_of, total, most, slope), jnp.int32)
    twos = (number_of - 1) // 2
    source_of, receiver = sizes[1:1 + 2 * twos:2], sizes[2:2 + 2 * twos:2]
    slack = jnp.minimum(source_of - 1, most - receiver)
    passed = jax.random.randint(jax.random.fold_in(rng, 1), (twos,), 0, 1 << 20) % (slack + 1)
    sizes = sizes.at[1:1 + 2 * twos:2].set(source_of - passed).at[2:2 + 2 * twos:2].set(receiver + passed)
    return sizes[jax.random.permutation(jax.random.fold_in(rng, 2), number_of)]


def centred(rng, shape, scale, reach, shards=(), kind=jnp.bfloat16):
    drawn = jax.random.normal(rng, shape, jnp.float32) * scale
    if len(shards) > 0:
        drawn = level_of(rng, shape, shards, -0.22, 0.18) * drawn
    return jnp.clip(drawn, min=-reach, max=reach).astype(kind)


def setup_inputs(seed: int = 0) -> dict:
    key_of = jax.random.split(jax.random.key(seed), 11)
    feats = centred(key_of[0], (ATOMS, C), 1.0, 6.0, ((0, 32),))
    coords = jnp.clip(1.0 * jax.random.uniform(key_of[1], (3, ATOMS), jnp.float32) ** level_of(key_of[1], (3, ATOMS), ((1, 32),), -0.2, 0.2), 0.0, 1.0)
    cell_ids = jax.vmap(lambda own: jnp.searchsorted(jnp.cumsum(uneven_parts(own, CELL_DEV, ATOM_DEV, MOST, 2)), jnp.arange(ATOM_DEV), side="right"))(jax.random.split(key_of[2], N_DP)).reshape((N_DP, ATOM_DEV)).astype(jnp.int32)
    recip = jnp.clip(0.05 + 0.29999999 * jax.random.uniform(key_of[3], (N_DP, CELL_DEV, 9), jnp.float32) ** level_of(key_of[3], (N_DP, CELL_DEV, 9), ((0, 32),), -0.2, 0.2), 0.05, 0.35)
    kvec = touch_ends(jax.random.randint(key_of[4], (3, K), -4, 5), jax.random.fold_in(key_of[4], 1), -4, 4).astype(jnp.int32)
    w_in = centred(key_of[5], (C, C), C ** -0.5, 0.375)
    w_out = centred(key_of[6], (C, C), C ** -0.5, 0.375)
    kfilt = centred(key_of[7], (K, C), 0.5, 3.0, ((0, 8),), jnp.float32)
    spread = jnp.clip(jnp.exp(jax.random.uniform(key_of[8], (C,), jnp.float32, math.log(0.02), math.log(0.5))), 0.02, 0.5)
    cotan = centred(key_of[9], (ATOMS, C), 1.0, 6.0, ((0, 32),))
    return dict(feats=feats, coords=coords, cell_ids=cell_ids, recip=recip, kvec=kvec, w_in=w_in, w_out=w_out, kfilt=kfilt, spread=spread, cotan=cotan)


TWO_PI = 6.283185307179586

def phases(fractional, lattice):
    indices = lattice.astype(jnp.float32)
    phase_angle = fractional[0][:, None] * indices[0][None, :] + fractional[1][:, None] * indices[1][None, :]
    phase_angle = TWO_PI * (phase_angle + fractional[2][:, None] * indices[2][None, :])
    return (jnp.cos(phase_angle).astype(jnp.bfloat16), jnp.sin(phase_angle).astype(jnp.bfloat16))

def envelope(recip_rows, lattice, spread):
    indices = lattice.astype(jnp.float32)
    squared = jnp.zeros((recip_rows.shape[0], indices.shape[1]), jnp.float32)
    for row_index in range(3):
        component = recip_rows[:, 3 * row_index][:, None] * indices[0][None, :]
        component = component + recip_rows[:, 3 * row_index + 1][:, None] * indices[1][None, :]
        component = component + recip_rows[:, 3 * row_index + 2][:, None] * indices[2][None, :]
        squared = squared + component * component
    return jnp.exp(-squared[:, :, None] * spread[None, None, :])

def silu_slope(values):
    sigma = jax.nn.sigmoid(values)
    return sigma * (1.0 + values * (1.0 - sigma))

def padded(table, extra):
    return jnp.concatenate([table, jnp.zeros((extra,) + table.shape[1:], table.dtype)], axis=0)

def cell_layout(cell_rows, cell_total):
    numbers = jnp.arange(cell_total, dtype=jnp.int32)
    counts = lax.optimization_barrier(jnp.sum((cell_rows[None, :] == numbers[:, None]).astype(jnp.int32), axis=1))
    offsets = lax.optimization_barrier(jnp.sum((cell_rows[None, :] < numbers[:, None]).astype(jnp.int32), axis=1))
    return (counts, offsets)

def structure_pass(projected, cosines, sines, cell_rows, filters):
    atom_count = projected.shape[0]
    counts, offsets = cell_layout(cell_rows, filters.shape[0])
    proj_pad = padded(projected, MOST)
    cos_pad = padded(cosines, MOST)
    sin_pad = padded(sines, MOST)
    rows_pad = jnp.concatenate([cell_rows, jnp.full((MOST,), -1, jnp.int32)])
    message = jnp.zeros((atom_count + MOST, projected.shape[1]), jnp.float32)
    real_parts = []
    imag_parts = []
    for cell_index in range(filters.shape[0]):
        offset = offsets[cell_index]
        member = lax.dynamic_slice_in_dim(rows_pad, offset, MOST, 0) == cell_index
        member_half = member.astype(jnp.bfloat16)[:, None]
        cos_rows = lax.dynamic_slice_in_dim(cos_pad, offset, MOST, 0)
        sin_rows = lax.dynamic_slice_in_dim(sin_pad, offset, MOST, 0)
        proj_rows = lax.dynamic_slice_in_dim(proj_pad, offset, MOST, 0)
        real_part = jnp.dot((cos_rows * member_half).T, proj_rows, preferred_element_type=jnp.float32)
        imag_part = jnp.dot((sin_rows * member_half).T, proj_rows, preferred_element_type=jnp.float32)
        scale = 1.0 / counts[cell_index].astype(jnp.float32)
        weight_re = (filters[cell_index] * real_part * scale).astype(jnp.bfloat16)
        weight_im = (filters[cell_index] * imag_part * scale).astype(jnp.bfloat16)
        contrib = jnp.dot(cos_rows, weight_re, preferred_element_type=jnp.float32)
        contrib = contrib + jnp.dot(sin_rows, weight_im, preferred_element_type=jnp.float32)
        contrib = contrib * member.astype(jnp.float32)[:, None]
        previous = lax.dynamic_slice_in_dim(message, offset, MOST, 0)
        message = lax.dynamic_update_slice_in_dim(message, previous + contrib, offset, 0)
        real_parts.append(real_part)
        imag_parts.append(imag_part)
    return (message[:atom_count], real_parts, imag_parts)

def adjoint_pass(message_grad, cosines, sines, cell_rows, filters, shapes, real_parts, imag_parts):
    atom_count = message_grad.shape[0]
    counts, offsets = cell_layout(cell_rows, filters.shape[0])
    grad_pad = padded(message_grad, MOST)
    cos_pad = padded(cosines, MOST)
    sin_pad = padded(sines, MOST)
    rows_pad = jnp.concatenate([cell_rows, jnp.full((MOST,), -1, jnp.int32)])
    update = jnp.zeros((atom_count + MOST, message_grad.shape[1]), jnp.float32)
    filter_grad = jnp.zeros(filters.shape[1:], jnp.float32)
    for cell_index in range(filters.shape[0]):
        offset = offsets[cell_index]
        member = lax.dynamic_slice_in_dim(rows_pad, offset, MOST, 0) == cell_index
        member_half = member.astype(jnp.bfloat16)[:, None]
        cos_rows = lax.dynamic_slice_in_dim(cos_pad, offset, MOST, 0)
        sin_rows = lax.dynamic_slice_in_dim(sin_pad, offset, MOST, 0)
        grad_rows = lax.dynamic_slice_in_dim(grad_pad, offset, MOST, 0)
        scale = 1.0 / counts[cell_index].astype(jnp.float32)
        back_re = jnp.dot((cos_rows * member_half).T, grad_rows, preferred_element_type=jnp.float32) * scale
        back_im = jnp.dot((sin_rows * member_half).T, grad_rows, preferred_element_type=jnp.float32) * scale
        source_re = (filters[cell_index] * back_re).astype(jnp.bfloat16)
        source_im = (filters[cell_index] * back_im).astype(jnp.bfloat16)
        contrib = jnp.dot(cos_rows, source_re, preferred_element_type=jnp.float32)
        contrib = contrib + jnp.dot(sin_rows, source_im, preferred_element_type=jnp.float32)
        contrib = contrib * member.astype(jnp.float32)[:, None]
        previous = lax.dynamic_slice_in_dim(update, offset, MOST, 0)
        update = lax.dynamic_update_slice_in_dim(update, previous + contrib, offset, 0)
        filter_grad = filter_grad + shapes[cell_index] * (real_parts[cell_index] * back_re + imag_parts[cell_index] * back_im)
    return (update[:atom_count], filter_grad)

def reference(feats, coords, cell_ids, recip, kvec, w_in, w_out, kfilt, spread, cotan):
    feat_blocks = feats.reshape(N_DP, ATOM_DEV, C)
    cot_blocks = cotan.reshape(N_DP, ATOM_DEV, C)
    frac_blocks = jnp.transpose(coords.reshape(3, N_DP, ATOM_DEV), (1, 0, 2))

    def one_block(carry, inputs):
        feat_rows, cot_rows, frac_rows, cell_rows, recip_rows = inputs
        projected = jnp.dot(feat_rows, w_in, preferred_element_type=jnp.float32).astype(jnp.bfloat16)
        cosines, sines = phases(frac_rows, kvec)
        shapes = envelope(recip_rows, kvec, spread)
        filters = kfilt[None] * shapes
        message, real_parts, imag_parts = structure_pass(projected, cosines, sines, cell_rows, filters)
        activated = jax.nn.silu(message).astype(jnp.bfloat16)
        mixed = (feat_rows.astype(jnp.float32) + jnp.dot(activated, w_out, preferred_element_type=jnp.float32)).astype(jnp.bfloat16)
        act_grad = jnp.dot(cot_rows, w_out.T, preferred_element_type=jnp.float32)
        message_grad = (act_grad * silu_slope(message)).astype(jnp.bfloat16)
        update, filter_grad = adjoint_pass(message_grad, cosines, sines, cell_rows, filters, shapes, real_parts, imag_parts)
        update = update.astype(jnp.bfloat16)
        feat_grad = (cot_rows.astype(jnp.float32) + jnp.dot(update, w_in.T, preferred_element_type=jnp.float32)).astype(jnp.bfloat16)
        grad_in = carry[0] + jnp.dot(feat_rows.T, update, preferred_element_type=jnp.float32)
        grad_out = carry[1] + jnp.dot(activated.T, cot_rows, preferred_element_type=jnp.float32)
        return ((grad_in, grad_out, carry[2] + filter_grad), (mixed, feat_grad))
    start_carry = (jnp.zeros((C, C), jnp.float32), jnp.zeros((C, C), jnp.float32), jnp.zeros(kfilt.shape, jnp.float32))
    sums, outputs = lax.scan(one_block, start_carry, (feat_blocks, cot_blocks, frac_blocks, cell_ids, recip))
    raw_in, raw_out, raw_kfilt = sums
    mean_weights = (jnp.sum(raw_in * raw_in) + jnp.sum(raw_out * raw_out)) / (2 * C * C)
    mean_filter = jnp.sum(raw_kfilt * raw_kfilt) / (raw_kfilt.shape[0] * C)
    weight_scale = lax.rsqrt(mean_weights + 1e-06)
    filter_scale = lax.rsqrt(mean_filter + 1e-06)
    mixed = outputs[0].reshape(N_DP * ATOM_DEV, C)
    feat_grad = outputs[1].reshape(N_DP * ATOM_DEV, C)
    return (mixed, feat_grad, raw_in * weight_scale, raw_out * weight_scale, raw_kfilt * filter_scale)
```

```python
import functools

import jax
import jax.numpy as jnp
from jax import lax
from jax.experimental import pallas as pl
from jax.experimental.pallas import tpu as pltpu
from jax.sharding import PartitionSpec as P

MESH = pl.DeviceIdType.MESH
F32, BF16 = jnp.float32, jnp.bfloat16
NT = (((1,), (1,)), ((), ()))
TN = (((0,), (0,)), ((), ()))
GATHER_VMEM, REDUCE_VMEM = 30 << 20, 30 << 20
POINTS = 384
DEPTHS = (256, 384, 512, 768, 1152)
HEIGHTS = (96, 160, 224, 320, 528, 784, 1040)
COS = (0.9999992251396179, -19.738981246948242, 64.92865753173828, -85.27162170410156, 58.79049301147461, -21.07110595703125)
SIN = (6.283185005187988, -41.341590881347656, 81.59994506835938, -76.61447143554688, 41.3428840637207, -12.471243858337402)


def poly(coefs, s):
    total = coefs[-1] * s + coefs[-2]
    for c in coefs[-3::-1]:
        total = total * s + c
    return total


def mm(a, b):
    return jnp.dot(a, b, preferred_element_type=F32)


def mm_nt(a, b):
    return lax.dot_general(a, b, NT, preferred_element_type=F32)


def mm_tn(a, b):
    return lax.dot_general(a, b, TN, preferred_element_type=F32)


def lattice(shape, axis):
    n = lax.broadcasted_iota(jnp.int32, shape, axis).astype(F32) + 364.0
    i = jnp.floor((n + 0.5) * (1.0 / 81.0))
    rest = n - 81.0 * i
    j = jnp.floor((rest + 0.5) * (1.0 / 9.0))
    return i - 4.0, j - 4.0, rest - 9.0 * j - 4.0


def point_of(k):
    return jnp.abs(81.0 * k[0:1] + 9.0 * k[1:2] + k[2:3])


def gather_kernel(
    n_ka, feats_in, coords_in, cells_in, recip_in, kvec_in, w_in_in, kfilt_in, spread_in, cotan_in, w_out_in,
    cs, ct, proj, back, shapes, kf, meta,
    feats, coords, own_cells, recip, kvec, w_in, kfilt, spread, cotan, w_out,
    high, low, loads, send, recv, p_send, p_recv,
):
    me, dp = lax.axis_index("ka"), lax.axis_index("dp")
    right, left = lax.rem(me + 1, n_ka), lax.rem(me + n_ka - 1, n_ka)
    core = lax.rem(dp, 2)
    twin = dp + 1 - 2 * core
    barrier = pltpu.get_barrier_semaphore()
    for peer in (left, right):
        pl.semaphore_signal(barrier, inc=1, device_id={"ka": peer}, device_id_type=MESH)
    pl.semaphore_signal(barrier, inc=1, device_id={"dp": twin}, device_id_type=MESH)
    pairs = (
        (kfilt_in, kfilt), (kvec_in, kvec), (coords_in, coords), (cells_in, own_cells), (w_in_in, w_in),
        (feats_in, feats), (recip_in, recip), (spread_in, spread), (w_out_in, w_out), (cotan_in, cotan),
    )
    loading = [pltpu.make_async_copy(a, b, loads.at[i]) for i, (a, b) in enumerate(pairs)]
    for c in loading:
        c.start()
    depth, chan = kfilt.shape
    part = depth // 2
    atoms = cs.shape[1]
    loading[0].wait()
    loading[1].wait()
    first = kfilt[...].astype(BF16)
    second = (kfilt[...] - first.astype(F32)).astype(BF16)
    kpad = jnp.concatenate([kvec[...].astype(F32), jnp.zeros((13, depth), F32)], axis=0)
    for h in range(2):
        rows = slice(h * part, (h + 1) * part)
        high[me, h, 0:part, :] = first[rows]
        low[me, h] = second[rows]
        k = kpad[:, rows]
        high[me, h, part:part + 16, :] = jnp.concatenate([k, k, k, k], axis=1).astype(BF16)
    pl.semaphore_wait(barrier, 3)

    hops = (n_ka // 2, n_ka - 1 - n_ka // 2)
    halves = (high, low)

    def hop(half, way, step):
        slot = lax.rem(me - step + n_ka, n_ka) if way == 0 else lax.rem(me + step, n_ka)
        ref = halves[half].at[slot, core]
        return pltpu.make_async_remote_copy(
            src_ref=ref, dst_ref=ref, send_sem=send.at[half, way, step], recv_sem=recv.at[half, way, step],
            device_id={"ka": right if way == 0 else left}, device_id_type=MESH,
        )

    def share(half, way, step):
        slot = lax.rem(me - step - 1 + n_ka, n_ka) if way == 0 else lax.rem(me + step + 1, n_ka)
        ref = halves[half].at[slot, core]
        return pltpu.make_async_remote_copy(
            src_ref=ref, dst_ref=ref, send_sem=p_send.at[half, way, step], recv_sem=p_recv.at[half, way, step],
            device_id={"dp": twin}, device_id_type=MESH,
        )

    def trig(i):
        at = pl.multiple_of(i * 16, 16)
        n = (lax.broadcasted_iota(jnp.int32, (16, 1), 0) + (at + 364)).astype(F32)
        kx = jnp.floor((n + 0.5) * (1.0 / 81.0))
        rest = n - 81.0 * kx
        ky = jnp.floor((rest + 0.5) * (1.0 / 9.0))
        kz = rest - 9.0 * ky - 4.0
        kx, ky = kx - 4.0, ky - 4.0
        for lane in range(0, atoms, 512):
            here = pl.ds(lane, 512)
            turn = (coords[0:1, here] * kx + coords[1:2, here] * ky) + coords[2:3, here] * kz
            turn = turn - jnp.round(turn)
            s = turn * turn
            cs[pl.ds(at, 16), here] = poly(COS, s).astype(BF16)
            cs[pl.ds(POINTS + at, 16), here] = (turn * poly(SIN, s)).astype(BF16)

    chunks = POINTS // 16
    split = chunks // 2

    def envelope():
        loading[3].wait()
        loading[6].wait()
        loading[7].wait()
        n_cells = recip.shape[1]
        own = own_cells[...]
        lane = lax.broadcasted_iota(jnp.int32, (1, 128), 1)
        info = jnp.zeros((1, 128), jnp.int32)
        kx, ky, kz = lattice((1, POINTS), 1)
        b = recip[0]
        q = jnp.zeros((n_cells, POINTS), F32)
        for r in range(3):
            dot = (b[:, 3 * r:3 * r + 1] * kx + b[:, 3 * r + 1:3 * r + 2] * ky) + b[:, 3 * r + 2:3 * r + 3] * kz
            q = q + dot * dot
        q = jnp.concatenate([q] + [jnp.zeros((128 - n_cells, POINTS), F32)], axis=0).T
        for i in range(n_cells):
            count = jnp.sum((own == i).astype(F32), axis=1, keepdims=True)
            before = jnp.sum((own < i).astype(F32), axis=1, keepdims=True)
            info = jnp.where(lane == i, before.astype(jnp.int32), info)
            info = jnp.where(lane == 8 + i, count.astype(jnp.int32), info)
            shapes[i] = jnp.exp(-(q[:, i:i + 1] * spread[...])) * (1.0 / count)
        meta[...] = info

    def stage(step):
        if step == 0:
            loading[4].wait()
            loading[5].wait()
            proj[...] = mm(feats[...], w_in[...]).astype(BF16)
            loading[2].wait()
            pl.loop(0, split)(trig)
        elif step == 1:
            pl.loop(split, chunks)(trig)
        elif step == 2:
            envelope()
            loading[8].wait()
            loading[9].wait()
            back[...] = mm_nt(cotan[...], w_out[...])
        else:
            for p in range(0, 2 * POINTS, 256):
                for a in range(0, atoms, 256):
                    ct[a:a + 256, p:p + 256] = cs[p:p + 256, a:a + 256].T

    pending, shared = [], []

    def ways(step):
        return [way for way in (0, 1) if 0 <= step < hops[way]]

    for step in range(hops[0] + 1):
        for half in (0, 1):
            for way in ways(step - 1):
                hop(half, way, step - 1).wait_recv()
            for way in ways(step):
                c = hop(half, way, step)
                c.start()
                pending.append(c)
            for way in ways(step - 1):
                c = share(half, way, step - 1)
                c.start()
                shared.append(c)
        if step < hops[0]:
            stage(step)
    for c in shared:
        c.wait_recv()
    point = lax.broadcasted_iota(jnp.int32, (POINTS, 2 * depth), 0).astype(F32)
    total = jnp.zeros((POINTS, chan), F32)
    for z in range(n_ka):
        k = jnp.concatenate([high[z, h, part:part + 16, 0:depth] for h in (0, 1)], axis=1).astype(F32)
        hot = (point == point_of(k)).astype(BF16)
        terms = jnp.concatenate([high[z, 0, 0:part, :], low[z, 0], high[z, 1, 0:part, :], low[z, 1]], axis=0)
        total = total + mm(hot, terms)
    kf[...] = total
    for c in pending + shared:
        c.wait_send()


def cell_kernel(meta, cs, ct, proj, back, shapes, kf, act, upd, rsum, pull, push, grad):
    atoms = cs.shape[1]
    half, other = pl.ds(0, POINTS), pl.ds(POINTS, POINTS)

    def windows(i, unit, sizes, run):
        off, n = meta[0, i], meta[0, 8 + i]
        base = lax.div(off, unit) * unit
        span = off + n - base
        low = 0
        for size in sizes:
            @pl.when((span > low) & (span <= size))
            def _():
                start = pl.multiple_of(jnp.minimum(base, atoms - size), unit)
                row = lax.broadcasted_iota(jnp.int32, (size, 1), 0) + start
                run(pl.ds(start, size), (row >= off) & (row < off + n))
            low = size

    def factors(source, target, i):
        def run(here, inside):
            picked = jnp.where(inside, source[here, :].astype(F32), 0.0).astype(BF16)
            target[...] = mm(cs[:, here], picked)
        windows(i, 128, DEPTHS, run)

    def fields(filt, terms, i, use):
        weights = jnp.concatenate([(filt * terms[half]).astype(BF16), (filt * terms[other]).astype(BF16)], axis=0)

        def run(here, inside):
            use(here, inside, mm(ct[here, :], weights))
        windows(i, 16, HEIGHTS, run)

    def keep(target, here, inside, new):
        target[here, :] = jnp.where(inside, new, target[here, :].astype(F32)).astype(BF16)

    def forward(here, inside, m):
        s = 0.5 * jnp.tanh(0.5 * m) + 0.5
        keep(act, here, inside, m * s)
        keep(grad, here, inside, back[here, :] * (s * (1.0 + m * (1.0 - s))))

    rsum[...] = jnp.zeros_like(rsum)

    @pl.loop(0, shapes.shape[0])
    def _(i):
        factors(proj, push, i)
        fields(shapes[i] * kf[...], push, i, forward)
        factors(grad, pull, i)
        shape = shapes[i]
        rsum[...] += shape * (push[half] * pull[half] + push[other] * pull[other])
        fields(shape * kf[...], pull, i, functools.partial(keep, upd))


def reduce_kernel(
    n_dp, n_ka, mean_weights, mean_filter, act, upd, rsum, feats_in, cotan_in, w_in_in, w_out_in, kvec_in,
    mixed, feat_grad, grad_in, grad_out, grad_filt,
    feats, cotan, w_in, w_out, kvec, raw, landed, gath, squares, sq_landed, sq_gath,
    loads, s_send, s_recv, g_send, g_recv, z_send, z_recv, q_send, q_recv,
):
    pairs = ((cotan_in, cotan), (feats_in, feats), (kvec_in, kvec), (w_out_in, w_out), (w_in_in, w_in))
    loading = [pltpu.make_async_copy(a, b, loads.at[i]) for i, (a, b) in enumerate(pairs)]
    for c in loading:
        c.start()
    me, ka = lax.axis_index("dp"), lax.axis_index("ka")
    chan = grad_in.shape[0]
    height = chan // n_dp
    barrier = pltpu.get_barrier_semaphore()

    def peer(i):
        return lax.rem(me + i, n_dp)

    @pl.loop(1, n_dp)
    def _(i):
        pl.semaphore_signal(barrier, inc=1, device_id={"dp": peer(i)}, device_id_type=MESH)

    @pl.loop(1, n_ka)
    def _(i):
        pl.semaphore_signal(barrier, inc=1, device_id={"ka": lax.rem(ka + i, n_ka)}, device_id_type=MESH)

    atoms, depth = act.shape[0], kvec.shape[1]
    for c in loading:
        c.wait()
    raw[:, :, 0:chan] = mm_tn(act[...], cotan[...]).reshape(n_dp, height, chan).astype(BF16)
    raw[:, :, chan:2 * chan] = mm_tn(feats[...], upd[...]).reshape(n_dp, height, chan).astype(BF16)
    point = lax.broadcasted_iota(jnp.int32, (POINTS, depth), 0).astype(F32)
    hot = (point == point_of(kvec[...].astype(F32))).astype(BF16).T
    rest = rsum[...]
    own = jnp.zeros((depth, chan), F32)
    for _ in range(3):
        piece = rest.astype(BF16)
        own = own + mm(hot, piece)
        rest = rest - piece.astype(F32)
    own = jnp.concatenate([own[:, 0:chan // 2], own[:, chan // 2:]], axis=0)
    raw[:, :, 2 * chan:] = own.reshape(n_dp, height, chan // 2).astype(BF16)
    pl.semaphore_wait(barrier, n_dp - 1 + n_ka - 1)

    def scatter(i):
        return pltpu.make_async_remote_copy(
            src_ref=raw.at[peer(i)], dst_ref=landed.at[i - 1], send_sem=s_send.at[i - 1], recv_sem=s_recv.at[i - 1],
            device_id={"dp": peer(i)}, device_id_type=MESH,
        )

    def gather(i):
        return pltpu.make_async_remote_copy(
            src_ref=gath.at[me], dst_ref=gath.at[me], send_sem=g_send.at[i - 1], recv_sem=g_recv.at[i - 1],
            device_id={"dp": peer(i)}, device_id_type=MESH,
        )

    def across(i):
        return pltpu.make_async_remote_copy(
            src_ref=squares, dst_ref=sq_landed.at[i - 1], send_sem=z_send.at[i - 1], recv_sem=z_recv.at[i - 1],
            device_id={"ka": lax.rem(ka + i, n_ka)}, device_id_type=MESH,
        )

    def gather_sq(i):
        return pltpu.make_async_remote_copy(
            src_ref=sq_gath.at[me], dst_ref=sq_gath.at[me], send_sem=q_send.at[i - 1], recv_sem=q_recv.at[i - 1],
            device_id={"dp": peer(i)}, device_id_type=MESH,
        )

    def each(copy, act, n):
        @pl.loop(1, n)
        def _(i):
            act(copy(i))

    each(scatter, lambda c: c.start(), n_dp)
    for a in range(0, atoms, 512):
        mixed[a:a + 512, :] = (feats[a:a + 512, :].astype(F32) + mm(act[a:a + 512, :], w_out[...])).astype(BF16)
    each(scatter, lambda c: c.wait_recv(), n_dp)
    total = raw[me].astype(F32)
    for i in range(n_dp - 1):
        total = total + landed[i].astype(F32)
    gath[me] = total.astype(BF16)
    each(gather, lambda c: c.start(), n_dp)
    tail = total[:, 2 * chan:]
    squares[...] = tail * tail
    each(across, lambda c: c.start(), n_ka)
    for a in range(0, atoms, 512):
        feat_grad[a:a + 512, :] = (cotan[a:a + 512, :].astype(F32) + mm_nt(upd[a:a + 512, :], w_in[...])).astype(BF16)
    each(across, lambda c: c.wait_recv(), n_ka)
    added = squares[...]
    for i in range(n_ka - 1):
        added = added + sq_landed[i]
    sq_gath[me] = added
    each(gather_sq, lambda c: c.start(), n_dp)
    each(gather, lambda c: c.wait_recv(), n_dp)
    everything = gath[...].astype(F32).reshape(chan, gath.shape[2])
    weights = everything[:, 0:2 * chan]
    scale = lax.rsqrt(jnp.sum(weights * weights, axis=(0, 1), keepdims=True) * mean_weights + 1e-06)
    grad_out[...] = everything[:, 0:chan] * scale
    grad_in[...] = everything[:, chan:2 * chan] * scale
    each(gather_sq, lambda c: c.wait_recv(), n_dp)
    summed = sq_gath[...].reshape(n_dp * height, sq_gath.shape[2])
    scale = lax.rsqrt(jnp.sum(summed, axis=(0, 1), keepdims=True) * mean_filter + 1e-06)
    tail = everything[:, 2 * chan:] * scale
    grad_filt[...] = jnp.concatenate([tail[0:depth], tail[depth:]], axis=1)
    each(scatter, lambda c: c.wait_send(), n_dp)
    each(gather, lambda c: c.wait_send(), n_dp)
    each(across, lambda c: c.wait_send(), n_ka)
    each(gather_sq, lambda c: c.wait_send(), n_dp)


def put_kernel(*refs):
    n = (len(refs) - 1) // 2
    copies = [pltpu.make_async_copy(refs[i], refs[n + i], refs[-1].at[i]) for i in range(n)]
    for c in copies:
        c.start()
    for c in copies:
        c.wait()


def solution(mesh):
    n_dp, n_ka = mesh.shape["dp"], mesh.shape["ka"]
    vmem = pl.BlockSpec(memory_space=pltpu.VMEM)
    smem = pl.BlockSpec(memory_space=pltpu.SMEM)
    hbm = pl.BlockSpec(memory_space=pltpu.HBM)
    dma = pltpu.SemaphoreType.DMA

    def body(feats, coords, cell_ids, recip, kvec, w_in, w_out, kfilt, spread, cotan):
        atoms, chan = feats.shape
        depth = kfilt.shape[0]
        cells = recip.shape[1]
        shape = jax.ShapeDtypeStruct
        height, width = chan // n_dp, 2 * chan + depth
        part = depth // 2
        spread = spread.reshape(1, chan)

        def far(*arrays):
            return [pltpu.with_memory_space_constraint(a, pltpu.HBM) for a in arrays]

        def held(*arrays):
            return [pltpu.VMEM(a.shape, a.dtype) for a in arrays]

        cs, ct, proj, back, shapes, kf, meta = pl.pallas_call(
            functools.partial(gather_kernel, n_ka),
            out_shape=(
                shape((2 * POINTS, atoms), BF16),
                shape((atoms, 2 * POINTS), BF16),
                shape((atoms, chan), BF16),
                shape((atoms, chan), F32),
                shape((cells, POINTS, chan), F32),
                shape((POINTS, chan), F32),
                shape((1, 128), jnp.int32),
            ),
            in_specs=[hbm] * 10,
            out_specs=[vmem] * 7,
            scratch_shapes=held(feats, coords, cell_ids, recip, kvec, w_in, kfilt, spread, cotan, w_out) + [
                pltpu.VMEM((n_ka, 2, part + 16, chan), BF16),
                pltpu.VMEM((n_ka, 2, part, chan), BF16),
                dma((10,)), dma((2, 2, n_ka)), dma((2, 2, n_ka)), dma((2, 2, n_ka)), dma((2, 2, n_ka)),
            ],
            compiler_params=pltpu.CompilerParams(collective_id=0, has_side_effects=True, vmem_limit_bytes=GATHER_VMEM),
            name="gather",
        )(*far(feats, coords, cell_ids, recip, kvec, w_in, kfilt, spread, cotan, w_out))
        act, upd, rsum = pl.pallas_call(
            cell_kernel,
            out_shape=(shape((atoms, chan), BF16), shape((atoms, chan), BF16), shape((POINTS, chan), F32)),
            in_specs=[smem] + [vmem] * 6,
            out_specs=[vmem] * 3,
            scratch_shapes=[
                pltpu.VMEM((2 * POINTS, chan), F32),
                pltpu.VMEM((2 * POINTS, chan), F32),
                pltpu.VMEM((atoms, chan), BF16),
            ],
            compiler_params=pltpu.CompilerParams(vmem_limit_bytes=24 << 20),
            name="cells",
        )(meta, cs, ct, proj, back, shapes, kf)
        results = pl.pallas_call(
            functools.partial(reduce_kernel, n_dp, n_ka, 1.0 / (2 * chan * chan), 1.0 / (depth * n_ka * chan)),
            out_shape=(
                shape((atoms, chan), BF16), shape((atoms, chan), BF16),
                shape((chan, chan), F32), shape((chan, chan), F32), shape((depth, chan), F32),
            ),
            in_specs=[vmem] * 3 + [hbm] * 5,
            out_specs=[vmem] * 5,
            scratch_shapes=held(feats, cotan, w_in, w_out, kvec) + [
                pltpu.VMEM((n_dp, height, width), BF16),
                pltpu.VMEM((n_dp - 1, height, width), BF16),
                pltpu.VMEM((n_dp, height, width), BF16),
                pltpu.VMEM((height, depth), F32),
                pltpu.VMEM((n_ka - 1, height, depth), F32),
                pltpu.VMEM((n_dp, height, depth), F32),
                dma((5,)), dma((n_dp,)), dma((n_dp,)), dma((n_dp,)), dma((n_dp,)),
                dma((n_ka,)), dma((n_ka,)), dma((n_dp,)), dma((n_dp,)),
            ],
            compiler_params=pltpu.CompilerParams(collective_id=1, has_side_effects=True, vmem_limit_bytes=REDUCE_VMEM),
            name="reduce",
        )(act, upd, rsum, feats, cotan, w_in, w_out, kvec)
        return tuple(pl.pallas_call(
            put_kernel,
            out_shape=[shape(r.shape, r.dtype) for r in results],
            in_specs=[vmem] * 5,
            out_specs=[hbm] * 5,
            scratch_shapes=[dma((5,))],
            compiler_params=pltpu.CompilerParams(vmem_limit_bytes=16 << 20),
            name="put",
        )(*results))

    placed = (
        P("dp", None), P(None, "dp"), P("dp", None), P("dp", None, None), P(None, "ka"),
        P(), P(), P("ka", None), P(), P("dp", None),
    )
    return jax.shard_map(
        body,
        mesh=mesh,
        in_specs=placed,
        out_specs=(P("dp", None), P("dp", None), P(), P(), P("ka", None)),
        check_vma=False,
    )
```

```python
import functools

import jax
import jax.numpy as jnp
from jax import lax
from jax.experimental import pallas as pl
from jax.experimental.pallas import tpu as pltpu
from jax.sharding import PartitionSpec as P

MESH = pl.DeviceIdType.MESH
F32, BF16 = jnp.float32, jnp.bfloat16
NT = (((1,), (1,)), ((), ()))
TN = (((0,), (0,)), ((), ()))
GATHER_VMEM, REDUCE_VMEM = 30 << 20, 24 << 20
POINTS = 384
DEPTHS = (256, 512, 768, 1152)
PIECES = {544: 2, 1040: 5}
HEIGHTS = (112, 176, 240, 320, 544, 1040)
COS = (0.9999992251396179, -19.738981246948242, 64.92865753173828, -85.27162170410156, 58.79049301147461, -21.07110595703125)
SIN = (6.283185005187988, -41.341590881347656, 81.59994506835938, -76.61447143554688, 41.3428840637207, -12.471243858337402)


def poly(coefs, s):
    total = coefs[-1] * s + coefs[-2]
    for c in coefs[-3::-1]:
        total = total * s + c
    return total


def mm(a, b):
    return jnp.dot(a, b, preferred_element_type=F32)


def mm_nt(a, b):
    return lax.dot_general(a, b, NT, preferred_element_type=F32)


def mm_tn(a, b):
    return lax.dot_general(a, b, TN, preferred_element_type=F32)


def lattice(shape, axis):
    n = lax.broadcasted_iota(jnp.int32, shape, axis).astype(F32) + 364.0
    i = jnp.floor((n + 0.5) * (1.0 / 81.0))
    rest = n - 81.0 * i
    j = jnp.floor((rest + 0.5) * (1.0 / 9.0))
    return i - 4.0, j - 4.0, rest - 9.0 * j - 4.0


def point_of(k):
    return jnp.abs(81.0 * k[0:1] + 9.0 * k[1:2] + k[2:3])


def gather_kernel(
    n_ka, feats_in, coords_in, cells_in, recip_in, kvec_in, w_in_in, kfilt_in, spread_in, cotan_in, w_out_in,
    cs, ct, proj, back, shapes, kf, meta,
    feats, coords, own_cells, recip, kvec, w_in, kfilt, spread, cotan, w_out,
    high, low, loads, send, recv, p_send, p_recv,
):
    me, dp = lax.axis_index("ka"), lax.axis_index("dp")
    right, left = lax.rem(me + 1, n_ka), lax.rem(me + n_ka - 1, n_ka)
    core = lax.rem(dp, 2)
    twin = dp + 1 - 2 * core
    barrier = pltpu.get_barrier_semaphore()
    for peer in (left, right):
        pl.semaphore_signal(barrier, inc=1, device_id={"ka": peer}, device_id_type=MESH)
    pl.semaphore_signal(barrier, inc=1, device_id={"dp": twin}, device_id_type=MESH)
    pairs = (
        (kfilt_in, kfilt), (kvec_in, kvec), (coords_in, coords), (cells_in, own_cells), (w_in_in, w_in),
        (feats_in, feats), (recip_in, recip), (spread_in, spread), (w_out_in, w_out), (cotan_in, cotan),
    )
    loading = [pltpu.make_async_copy(a, b, loads.at[i]) for i, (a, b) in enumerate(pairs)]
    for c in loading:
        c.start()
    depth, chan = kfilt.shape
    part = depth // 2
    atoms = cs.shape[1]
    loading[0].wait()
    loading[1].wait()
    first = kfilt[...].astype(BF16)
    second = (kfilt[...] - first.astype(F32)).astype(BF16)
    kpad = jnp.concatenate([kvec[...].astype(F32), jnp.zeros((13, depth), F32)], axis=0)
    for h in range(2):
        rows = slice(h * part, (h + 1) * part)
        high[me, h, 0:part, :] = first[rows]
        low[me, h] = second[rows]
        k = kpad[:, rows]
        high[me, h, part:part + 16, :] = jnp.concatenate([k, k, k, k], axis=1).astype(BF16)
    pl.semaphore_wait(barrier, 3)

    hops = (n_ka // 2, n_ka - 1 - n_ka // 2)
    halves = (high, low)

    def hop(half, way, step):
        slot = lax.rem(me - step + n_ka, n_ka) if way == 0 else lax.rem(me + step, n_ka)
        ref = halves[half].at[slot, core]
        return pltpu.make_async_remote_copy(
            src_ref=ref, dst_ref=ref, send_sem=send.at[half, way, step], recv_sem=recv.at[half, way, step],
            device_id={"ka": right if way == 0 else left}, device_id_type=MESH,
        )

    def share(half, way, step):
        slot = lax.rem(me - step - 1 + n_ka, n_ka) if way == 0 else lax.rem(me + step + 1, n_ka)
        ref = halves[half].at[slot, core]
        return pltpu.make_async_remote_copy(
            src_ref=ref, dst_ref=ref, send_sem=p_send.at[half, way, step], recv_sem=p_recv.at[half, way, step],
            device_id={"dp": twin}, device_id_type=MESH,
        )

    def trig(i):
        at = pl.multiple_of(i * 16, 16)
        n = (lax.broadcasted_iota(jnp.int32, (16, 1), 0) + (at + 364)).astype(F32)
        kx = jnp.floor((n + 0.5) * (1.0 / 81.0))
        rest = n - 81.0 * kx
        ky = jnp.floor((rest + 0.5) * (1.0 / 9.0))
        kz = rest - 9.0 * ky - 4.0
        kx, ky = kx - 4.0, ky - 4.0
        for lane in range(0, atoms, 512):
            here = pl.ds(lane, 512)
            turn = (coords[0:1, here] * kx + coords[1:2, here] * ky) + coords[2:3, here] * kz
            turn = turn - jnp.round(turn)
            s = turn * turn
            cs[pl.ds(at, 16), here] = poly(COS, s).astype(BF16)
            cs[pl.ds(POINTS + at, 16), here] = (turn * poly(SIN, s)).astype(BF16)

    chunks = POINTS // 16

    def envelope():
        loading[3].wait()
        loading[6].wait()
        loading[7].wait()
        n_cells = recip.shape[1]
        own = own_cells[...]
        lane = lax.broadcasted_iota(jnp.int32, (1, 128), 1)
        info = jnp.zeros((1, 128), jnp.int32)
        kx, ky, kz = lattice((1, POINTS), 1)
        b = recip[0]
        q = jnp.zeros((n_cells, POINTS), F32)
        for r in range(3):
            dot = (b[:, 3 * r:3 * r + 1] * kx + b[:, 3 * r + 1:3 * r + 2] * ky) + b[:, 3 * r + 2:3 * r + 3] * kz
            q = q + dot * dot
        q = jnp.concatenate([q] + [jnp.zeros((128 - n_cells, POINTS), F32)], axis=0).T
        for i in range(n_cells):
            count = jnp.sum((own == i).astype(F32), axis=1, keepdims=True)
            before = jnp.sum((own < i).astype(F32), axis=1, keepdims=True)
            info = jnp.where(lane == i, before.astype(jnp.int32), info)
            info = jnp.where(lane == 8 + i, count.astype(jnp.int32), info)
            shapes[i] = jnp.exp(-(q[:, i:i + 1] * spread[...])) * (1.0 / count)
        meta[...] = info

    pending, shared = [], []

    def ways(step):
        return [way for way in (0, 1) if 0 <= step < hops[way]]

    def slots_of(step):
        return [lax.rem(me + n_ka - step - 1, n_ka) if way == 0 else lax.rem(me + step + 1, n_ka) for way in ways(step)]

    def arrived(step):
        for half in (0, 1):
            for way in ways(step - 1):
                share(half, way, step - 1).wait_recv()

    def filter_of(slots):
        point = lax.broadcasted_iota(jnp.int32, (POINTS, 2 * depth), 0).astype(F32)
        total = None
        for z in slots:
            k = jnp.concatenate([high[z, h, part:part + 16, 0:depth] for h in (0, 1)], axis=1).astype(F32)
            hot = (point == point_of(k)).astype(BF16)
            terms = jnp.concatenate([high[z, 0, 0:part, :], low[z, 0], high[z, 1, 0:part, :], low[z, 1]], axis=0)
            new = mm(hot, terms)
            total = new if total is None else total + new
        if len(slots) == 1:
            kf[...] = total
        else:
            kf[...] += total

    def stage(step):
        if step == 0:
            loading[4].wait()
            loading[5].wait()
            proj[...] = mm(feats[...], w_in[...]).astype(BF16)
            loading[2].wait()
            pl.loop(0, 10)(trig)
        elif step == 1:
            filter_of([me])
            pl.loop(10, 21)(trig)
        elif step == 2:
            pl.loop(21, chunks)(trig)
            envelope()
            loading[8].wait()
            loading[9].wait()
            back[...] = mm_nt(cotan[...], w_out[...])
        else:
            arrived(1)
            filter_of(slots_of(0))
            for p in range(0, 2 * POINTS, 256):
                for a in range(0, atoms, 256):
                    ct[a:a + 256, p:p + 256] = cs[p:p + 256, a:a + 256].T


    for step in range(hops[0] + 1):
        for half in (0, 1):
            for way in ways(step - 1):
                hop(half, way, step - 1).wait_recv()
            for way in ways(step):
                c = hop(half, way, step)
                c.start()
                pending.append(c)
            for way in ways(step - 1):
                c = share(half, way, step - 1)
                c.start()
                shared.append(c)
        if step < hops[0]:
            stage(step)
    for step in (2, 3, 4):
        arrived(step)
    filter_of(slots_of(1) + slots_of(2) + slots_of(3))
    for c in pending + shared:
        c.wait_send()


def cell_kernel(meta, cs, ct, proj, back, shapes, kf, act, upd, pushes, pulls, grad, weights):
    atoms = cs.shape[1]
    half, other = pl.ds(0, POINTS), pl.ds(POINTS, POINTS)

    def windows(i, unit, sizes, run):
        off, n = meta[0, i], meta[0, 8 + i]
        base = lax.div(off, unit) * unit
        span = off + n - base
        low = 0
        for size in sizes:
            @pl.when((span > low) & (span <= size))
            def _():
                start = pl.multiple_of(jnp.minimum(base, atoms - size), unit)
                row = lax.broadcasted_iota(jnp.int32, (size, 1), 0) + start
                run(pl.ds(start, size), (row >= off) & (row < off + n))
            low = size

    def factors(source, target, i):
        def run(here, inside):
            rows = source[here, :]
            picked = jnp.where(inside, rows, jnp.zeros_like(rows))
            total = mm(cs[:, here], picked)
            target[...] = total
            filt = shapes[i] * kf[...]
            weights[half] = (filt * total[0:POINTS]).astype(BF16)
            weights[other] = (filt * total[POINTS:]).astype(BF16)
        windows(i, 128, DEPTHS, run)

    def fields(i, use):
        def run(here, inside):
            size = inside.shape[0]
            pieces = PIECES.get(size, 1)
            for n in range(pieces):
                at, step = n * (size // pieces), size // pieces
                rows = pl.ds(pl.multiple_of(here.start + at, 16), step)
                use(rows, inside[at:at + step], mm(ct[rows, :], weights[...]))
        windows(i, 16, HEIGHTS, run)

    def keep(target, here, inside, new):
        target[here, :] = jnp.where(inside, new.astype(BF16), target[here, :])

    def forward(here, inside, m):
        s = 0.5 * jnp.tanh(0.5 * m) + 0.5
        value = m * s
        keep(act, here, inside, value)
        keep(grad, here, inside, back[here, :] * (s + value * (1.0 - s)))

    @pl.loop(0, shapes.shape[0])
    def _(i):
        push, pull = pushes.at[i], pulls.at[i]
        factors(proj, push, i)
        fields(i, forward)
        factors(grad, pull, i)
        fields(i, functools.partial(keep, upd))


def reduce_kernel(
    n_dp, n_ka, mean_weights, mean_filter, act, upd, pushes, pulls, shapes, feats, cotan, w_in, w_out, kvec,
    mixed, feat_grad, grad_in, grad_out, grad_filt,
    filt, filt_landed, filt_gath, raw, landed, gath, squares, sq_landed, sq_gath,
    f_send, f_recv, h_send, h_recv, s_send, s_recv, g_send, g_recv, z_send, z_recv, q_send, q_recv,
):
    me, ka = lax.axis_index("dp"), lax.axis_index("ka")
    chan = grad_in.shape[0]
    height = chan // n_dp
    barrier = pltpu.get_barrier_semaphore()

    def peer(i):
        return lax.rem(me + i, n_dp)

    @pl.loop(1, n_dp)
    def _(i):
        pl.semaphore_signal(barrier, inc=1, device_id={"dp": peer(i)}, device_id_type=MESH)

    @pl.loop(1, n_ka)
    def _(i):
        pl.semaphore_signal(barrier, inc=1, device_id={"ka": lax.rem(ka + i, n_ka)}, device_id_type=MESH)

    def scatter(source, target, sends, receives):
        return lambda i: pltpu.make_async_remote_copy(
            src_ref=source.at[peer(i)], dst_ref=target.at[i - 1], send_sem=sends.at[i - 1], recv_sem=receives.at[i - 1],
            device_id={"dp": peer(i)}, device_id_type=MESH,
        )

    def gather(ref, sends, receives):
        return lambda i: pltpu.make_async_remote_copy(
            src_ref=ref.at[me], dst_ref=ref.at[me], send_sem=sends.at[i - 1], recv_sem=receives.at[i - 1],
            device_id={"dp": peer(i)}, device_id_type=MESH,
        )

    def across(i):
        return pltpu.make_async_remote_copy(
            src_ref=squares, dst_ref=sq_landed.at[i - 1], send_sem=z_send.at[i - 1], recv_sem=z_recv.at[i - 1],
            device_id={"ka": lax.rem(ka + i, n_ka)}, device_id_type=MESH,
        )

    scatter_filt = scatter(filt, filt_landed, f_send, f_recv)
    gather_filt = gather(filt_gath, h_send, h_recv)
    scatter_raw = scatter(raw, landed, s_send, s_recv)
    gather_raw = gather(gath, g_send, g_recv)
    gather_sq = gather(sq_gath, q_send, q_recv)

    def each(copy, act_on, n):
        @pl.loop(1, n)
        def _(i):
            act_on(copy(i))

    def start(c):
        c.start()

    def wait_recv(c):
        c.wait_recv()

    def wait_send(c):
        c.wait_send()

    def added(own, others):
        total = own.astype(F32)
        for i in range(others.shape[0]):
            total = total + others[i].astype(F32)
        return total

    atoms, depth = act.shape[0], kvec.shape[1]
    point = lax.broadcasted_iota(jnp.int32, (POINTS, depth), 0).astype(F32)
    hot = (point == point_of(kvec[...].astype(F32))).astype(BF16).T
    half, other = pl.ds(0, POINTS), pl.ds(POINTS, POINTS)
    rest = jnp.zeros((POINTS, chan), F32)
    for i in range(shapes.shape[0]):
        rest = rest + shapes[i] * (pushes[i, half] * pulls[i, half] + pushes[i, other] * pulls[i, other])
    own = jnp.zeros((depth, chan), F32)
    for _ in range(3):
        piece = rest.astype(BF16)
        own = own + mm(hot, piece)
        rest = rest - piece.astype(F32)
    own = jnp.concatenate([own[:, 0:chan // 2], own[:, chan // 2:]], axis=0)
    filt[...] = own.reshape(n_dp, height, chan // 2).astype(BF16)
    pl.semaphore_wait(barrier, n_dp - 1 + n_ka - 1)
    each(scatter_filt, start, n_dp)
    raw[:, :, 0:chan] = mm_tn(act[...], cotan[...]).reshape(n_dp, height, chan).astype(BF16)
    raw[:, :, chan:2 * chan] = mm_tn(feats[...], upd[...]).reshape(n_dp, height, chan).astype(BF16)
    each(scatter_raw, start, n_dp)
    for a in range(0, atoms, 512):
        mixed[a:a + 512, :] = (feats[a:a + 512, :].astype(F32) + mm(act[a:a + 512, :], w_out[...])).astype(BF16)
    each(scatter_filt, wait_recv, n_dp)
    total = added(filt[me], filt_landed)
    squares[...] = jnp.sum(total * total, axis=0, keepdims=True)
    each(across, start, n_ka)
    filt_gath[me] = total.astype(BF16)
    each(gather_filt, start, n_dp)
    each(scatter_raw, wait_recv, n_dp)
    gath[me] = added(raw[me], landed).astype(BF16)
    each(gather_raw, start, n_dp)
    each(across, wait_recv, n_ka)
    sq_gath[me] = added(squares[...], sq_landed)
    each(gather_sq, start, n_dp)
    for a in range(0, atoms, 512):
        feat_grad[a:a + 512, :] = (cotan[a:a + 512, :].astype(F32) + mm_nt(upd[a:a + 512, :], w_in[...])).astype(BF16)
    each(gather_filt, wait_recv, n_dp)
    each(gather_sq, wait_recv, n_dp)
    summed = sq_gath[...].reshape(n_dp, sq_gath.shape[2])
    scale = lax.rsqrt(jnp.sum(summed, axis=(0, 1), keepdims=True) * mean_filter + 1e-06)
    tail = filt_gath[...].astype(F32).reshape(chan, chan // 2) * scale
    grad_filt[...] = jnp.concatenate([tail[0:depth], tail[depth:]], axis=1)
    each(gather_raw, wait_recv, n_dp)
    weights = gath[...].astype(F32).reshape(chan, 2 * chan)
    scale = lax.rsqrt(jnp.sum(weights * weights, axis=(0, 1), keepdims=True) * mean_weights + 1e-06)
    grad_out[...] = weights[:, 0:chan] * scale
    grad_in[...] = weights[:, chan:] * scale
    for c in (scatter_filt, gather_filt, scatter_raw, gather_raw, gather_sq):
        each(c, wait_send, n_dp)
    each(across, wait_send, n_ka)


def put_kernel(*refs):
    n = (len(refs) - 1) // 2
    copies = [pltpu.make_async_copy(refs[i], refs[n + i], refs[-1].at[i]) for i in range(n)]
    for c in copies:
        c.start()
    for c in copies:
        c.wait()


def solution(mesh):
    n_dp, n_ka = mesh.shape["dp"], mesh.shape["ka"]
    vmem = pl.BlockSpec(memory_space=pltpu.VMEM)
    smem = pl.BlockSpec(memory_space=pltpu.SMEM)
    hbm = pl.BlockSpec(memory_space=pltpu.HBM)
    dma = pltpu.SemaphoreType.DMA

    def body(feats, coords, cell_ids, recip, kvec, w_in, w_out, kfilt, spread, cotan):
        atoms, chan = feats.shape
        depth = kfilt.shape[0]
        cells = recip.shape[1]
        shape = jax.ShapeDtypeStruct
        height = chan // n_dp
        part = depth // 2
        spread = spread.reshape(1, chan)

        def far(*arrays):
            return [pltpu.with_memory_space_constraint(a, pltpu.HBM) for a in arrays]

        def held(*arrays):
            return [pltpu.VMEM(a.shape, a.dtype) for a in arrays]

        cs, ct, proj, back, shapes, kf, meta = pl.pallas_call(
            functools.partial(gather_kernel, n_ka),
            out_shape=(
                shape((2 * POINTS, atoms), BF16),
                shape((atoms, 2 * POINTS), BF16),
                shape((atoms, chan), BF16),
                shape((atoms, chan), F32),
                shape((cells, POINTS, chan), F32),
                shape((POINTS, chan), F32),
                shape((1, 128), jnp.int32),
            ),
            in_specs=[hbm] * 10,
            out_specs=[vmem] * 7,
            scratch_shapes=held(feats, coords, cell_ids, recip, kvec, w_in, kfilt, spread, cotan, w_out) + [
                pltpu.VMEM((n_ka, 2, part + 16, chan), BF16),
                pltpu.VMEM((n_ka, 2, part, chan), BF16),
                dma((10,)), dma((2, 2, n_ka)), dma((2, 2, n_ka)), dma((2, 2, n_ka)), dma((2, 2, n_ka)),
            ],
            compiler_params=pltpu.CompilerParams(collective_id=0, has_side_effects=True, vmem_limit_bytes=GATHER_VMEM),
            name="gather",
        )(*far(feats, coords, cell_ids, recip, kvec, w_in, kfilt, spread, cotan, w_out))
        act, upd, pushes, pulls = pl.pallas_call(
            cell_kernel,
            out_shape=(
                shape((atoms, chan), BF16),
                shape((atoms, chan), BF16),
                shape((cells, 2 * POINTS, chan), F32),
                shape((cells, 2 * POINTS, chan), F32),
            ),
            in_specs=[smem] + [vmem] * 6,
            out_specs=[vmem] * 4,
            scratch_shapes=[pltpu.VMEM((atoms, chan), BF16), pltpu.VMEM((2 * POINTS, chan), BF16)],
            compiler_params=pltpu.CompilerParams(vmem_limit_bytes=16 << 20),
            name="cells",
        )(meta, cs, ct, proj, back, shapes, kf)
        results = pl.pallas_call(
            functools.partial(reduce_kernel, n_dp, n_ka, 1.0 / (2 * chan * chan), 1.0 / (depth * n_ka * chan)),
            out_shape=(
                shape((atoms, chan), BF16), shape((atoms, chan), BF16),
                shape((chan, chan), F32), shape((chan, chan), F32), shape((depth, chan), F32),
            ),
            in_specs=[vmem] * 10,
            out_specs=[vmem] * 5,
            scratch_shapes=[
                pltpu.VMEM((n_dp, height, chan // 2), BF16),
                pltpu.VMEM((n_dp - 1, height, chan // 2), BF16),
                pltpu.VMEM((n_dp, height, chan // 2), BF16),
                pltpu.VMEM((n_dp, height, 2 * chan), BF16),
                pltpu.VMEM((n_dp - 1, height, 2 * chan), BF16),
                pltpu.VMEM((n_dp, height, 2 * chan), BF16),
                pltpu.VMEM((1, chan // 2), F32),
                pltpu.VMEM((n_ka - 1, 1, chan // 2), F32),
                pltpu.VMEM((n_dp, 1, chan // 2), F32),
            ] + [dma((n_dp,))] * 8 + [dma((n_ka,))] * 2 + [dma((n_dp,))] * 2,
            compiler_params=pltpu.CompilerParams(collective_id=1, has_side_effects=True, vmem_limit_bytes=REDUCE_VMEM),
            name="reduce",
        )(act, upd, pushes, pulls, shapes, feats, cotan, w_in, w_out, kvec)
        return tuple(pl.pallas_call(
            put_kernel,
            out_shape=[shape(r.shape, r.dtype) for r in results],
            in_specs=[vmem] * 5,
            out_specs=[hbm] * 5,
            scratch_shapes=[dma((5,))],
            compiler_params=pltpu.CompilerParams(vmem_limit_bytes=16 << 20),
            name="put",
        )(*results))

    placed = (
        P("dp", None), P(None, "dp"), P("dp", None), P("dp", None, None), P(None, "ka"),
        P(), P(), P("ka", None), P(), P("dp", None),
    )
    return jax.shard_map(
        body,
        mesh=mesh,
        in_specs=placed,
        out_specs=(P("dp", None), P("dp", None), P(), P(), P("ka", None)),
        check_vma=False,
    )
```

```python
import functools

import jax
import jax.numpy as jnp
from jax import lax
from jax.experimental import pallas as pl
from jax.experimental.pallas import tpu as pltpu
from jax.sharding import PartitionSpec as P

MESH = pl.DeviceIdType.MESH
F32, BF16 = jnp.float32, jnp.bfloat16
NT = (((1,), (1,)), ((), ()))
TN = (((0,), (0,)), ((), ()))
GATHER_VMEM, REDUCE_VMEM = 30 << 20, 24 << 20
POINTS = 384
DEPTHS = (256, 512, 768, 1152)
PIECES = {544: 2, 1040: 5}
HEIGHTS = (112, 176, 240, 320, 544, 1040)
COS = (0.9999992251396179, -19.738981246948242, 64.92865753173828, -85.27162170410156, 58.79049301147461, -21.07110595703125)
SIN = (6.283185005187988, -41.341590881347656, 81.59994506835938, -76.61447143554688, 41.3428840637207, -12.471243858337402)


def poly(coefs, s):
    total = coefs[-1] * s + coefs[-2]
    for c in coefs[-3::-1]:
        total = total * s + c
    return total


def mm(a, b):
    return jnp.dot(a, b, preferred_element_type=F32)


def mm_nt(a, b):
    return lax.dot_general(a, b, NT, preferred_element_type=F32)


def mm_tn(a, b):
    return lax.dot_general(a, b, TN, preferred_element_type=F32)


def lattice(shape, axis):
    n = lax.broadcasted_iota(jnp.int32, shape, axis).astype(F32) + 364.0
    i = jnp.floor((n + 0.5) * (1.0 / 81.0))
    rest = n - 81.0 * i
    j = jnp.floor((rest + 0.5) * (1.0 / 9.0))
    return i - 4.0, j - 4.0, rest - 9.0 * j - 4.0


def point_of(k):
    return jnp.abs(81.0 * k[0:1] + 9.0 * k[1:2] + k[2:3])


def gather_kernel(
    n_ka, feats_in, coords_in, cells_in, recip_in, kvec_in, w_in_in, kfilt_in, spread_in, cotan_in, w_out_in,
    cs, ct, proj, back, shapes, kf, meta,
    feats, coords, own_cells, recip, kvec, w_in, kfilt, spread, cotan, w_out,
    high, low, loads, send, recv, p_send, p_recv,
):
    me, dp = lax.axis_index("ka"), lax.axis_index("dp")
    right, left = lax.rem(me + 1, n_ka), lax.rem(me + n_ka - 1, n_ka)
    core = lax.rem(dp, 2)
    twin = dp + 1 - 2 * core
    barrier = pltpu.get_barrier_semaphore()
    for peer in (left, right):
        pl.semaphore_signal(barrier, inc=1, device_id={"ka": peer}, device_id_type=MESH)
    pl.semaphore_signal(barrier, inc=1, device_id={"dp": twin}, device_id_type=MESH)
    pairs = (
        (kfilt_in, kfilt), (kvec_in, kvec), (coords_in, coords), (cells_in, own_cells), (w_in_in, w_in),
        (feats_in, feats), (recip_in, recip), (spread_in, spread), (w_out_in, w_out), (cotan_in, cotan),
    )
    loading = [pltpu.make_async_copy(a, b, loads.at[i]) for i, (a, b) in enumerate(pairs)]
    for c in loading:
        c.start()
    depth, chan = kfilt.shape
    part = depth // 2
    atoms = cs.shape[1]
    loading[0].wait()
    loading[1].wait()
    first = kfilt[...].astype(BF16)
    second = (kfilt[...] - first.astype(F32)).astype(BF16)
    kpad = jnp.concatenate([kvec[...].astype(F32), jnp.zeros((5, depth), F32)], axis=0)
    for h in range(2):
        rows = slice(h * part, (h + 1) * part)
        high[me, h, 0:part, :] = first[rows]
        low[me, h] = second[rows]
        k = kpad[:, rows]
        high[me, h, part:part + 8, :] = jnp.concatenate([k, k, k, k], axis=1).astype(BF16)
    pl.semaphore_wait(barrier, 3)

    hops = (n_ka // 2, n_ka - 1 - n_ka // 2)
    halves = (high, low)

    def hop(half, way, step):
        slot = lax.rem(me - step + n_ka, n_ka) if way == 0 else lax.rem(me + step, n_ka)
        ref = halves[half].at[slot, core]
        return pltpu.make_async_remote_copy(
            src_ref=ref, dst_ref=ref, send_sem=send.at[half, way, step], recv_sem=recv.at[half, way, step],
            device_id={"ka": right if way == 0 else left}, device_id_type=MESH,
        )

    def share(half, way, step):
        slot = lax.rem(me - step - 1 + n_ka, n_ka) if way == 0 else lax.rem(me + step + 1, n_ka)
        ref = halves[half].at[slot, core]
        return pltpu.make_async_remote_copy(
            src_ref=ref, dst_ref=ref, send_sem=p_send.at[half, way, step], recv_sem=p_recv.at[half, way, step],
            device_id={"dp": twin}, device_id_type=MESH,
        )

    def trig(i):
        at = pl.multiple_of(i * 16, 16)
        n = (lax.broadcasted_iota(jnp.int32, (16, 1), 0) + (at + 364)).astype(F32)
        kx = jnp.floor((n + 0.5) * (1.0 / 81.0))
        rest = n - 81.0 * kx
        ky = jnp.floor((rest + 0.5) * (1.0 / 9.0))
        kz = rest - 9.0 * ky - 4.0
        kx, ky = kx - 4.0, ky - 4.0
        for lane in range(0, atoms, 512):
            here = pl.ds(lane, 512)
            turn = (coords[0:1, here] * kx + coords[1:2, here] * ky) + coords[2:3, here] * kz
            turn = turn - jnp.round(turn)
            s = turn * turn
            cs[pl.ds(at, 16), here] = poly(COS, s).astype(BF16)
            cs[pl.ds(POINTS + at, 16), here] = (turn * poly(SIN, s)).astype(BF16)

    chunks = POINTS // 16

    def envelope():
        loading[3].wait()
        loading[6].wait()
        loading[7].wait()
        n_cells = recip.shape[1]
        own = own_cells[...]
        lane = lax.broadcasted_iota(jnp.int32, (1, 128), 1)
        info = jnp.zeros((1, 128), jnp.int32)
        kx, ky, kz = lattice((1, POINTS), 1)
        b = recip[0]
        q = jnp.zeros((n_cells, POINTS), F32)
        for r in range(3):
            dot = (b[:, 3 * r:3 * r + 1] * kx + b[:, 3 * r + 1:3 * r + 2] * ky) + b[:, 3 * r + 2:3 * r + 3] * kz
            q = q + dot * dot
        q = jnp.concatenate([q] + [jnp.zeros((128 - n_cells, POINTS), F32)], axis=0).T
        for i in range(n_cells):
            count = jnp.sum((own == i).astype(F32), axis=1, keepdims=True)
            before = jnp.sum((own < i).astype(F32), axis=1, keepdims=True)
            info = jnp.where(lane == i, before.astype(jnp.int32), info)
            info = jnp.where(lane == 8 + i, count.astype(jnp.int32), info)
            shapes[i] = jnp.exp(-(q[:, i:i + 1] * spread[...])) * (1.0 / count)
        meta[...] = info

    pending, shared = [], []

    def ways(step):
        return [way for way in (0, 1) if 0 <= step < hops[way]]

    def slots_of(step):
        return [lax.rem(me + n_ka - step - 1, n_ka) if way == 0 else lax.rem(me + step + 1, n_ka) for way in ways(step)]

    def arrived(step):
        for half in (0, 1):
            for way in ways(step - 1):
                share(half, way, step - 1).wait_recv()

    def filter_of(slots, begin=False):
        point = lax.broadcasted_iota(jnp.int32, (POINTS, 2 * depth), 0).astype(F32)
        total = None
        for z in slots:
            k = jnp.concatenate([high[z, h, part:part + 8, 0:depth] for h in (0, 1)], axis=1).astype(F32)
            hot = (point == point_of(k)).astype(BF16)
            terms = jnp.concatenate([high[z, 0, 0:part, :], low[z, 0], high[z, 1, 0:part, :], low[z, 1]], axis=0)
            new = mm(hot, terms)
            total = new if total is None else total + new
        if begin:
            kf[...] = total
        else:
            kf[...] += total

    def stage(step):
        if step == 0:
            loading[4].wait()
            loading[5].wait()
            proj[...] = mm(feats[...], w_in[...]).astype(BF16)
            loading[2].wait()
            pl.loop(0, 10)(trig)
        elif step == 1:
            filter_of([me], True)
            pl.loop(10, 21)(trig)
        elif step == 2:
            pl.loop(21, chunks)(trig)
            envelope()
            loading[8].wait()
            loading[9].wait()
            back[...] = mm_nt(cotan[...], w_out[...])
        else:
            arrived(1)
            filter_of(slots_of(0))
            for p in range(0, 2 * POINTS, 256):
                for a in range(0, atoms, 256):
                    ct[a:a + 256, p:p + 256] = cs[p:p + 256, a:a + 256].T
            arrived(2)
            filter_of(slots_of(1))


    for step in range(hops[0] + 1):
        for half in (0, 1):
            for way in ways(step - 1):
                hop(half, way, step - 1).wait_recv()
            for way in ways(step):
                c = hop(half, way, step)
                c.start()
                pending.append(c)
            for way in ways(step - 1):
                c = share(half, way, step - 1)
                c.start()
                shared.append(c)
        if step < hops[0]:
            stage(step)
    for step in (3, 4):
        arrived(step)
        filter_of(slots_of(step - 1))
    for c in pending + shared:
        c.wait_send()


def cell_kernel(meta, cs, ct, proj, back, shapes, kf, act, upd, pushes, pulls, grad, weights):
    atoms = cs.shape[1]
    half, other = pl.ds(0, POINTS), pl.ds(POINTS, POINTS)

    def windows(i, unit, sizes, run):
        off, n = meta[0, i], meta[0, 8 + i]
        base = lax.div(off, unit) * unit
        span = off + n - base
        low = 0
        for size in sizes:
            @pl.when((span > low) & (span <= size))
            def _():
                start = pl.multiple_of(jnp.minimum(base, atoms - size), unit)
                row = lax.broadcasted_iota(jnp.int32, (size, 1), 0) + start
                run(pl.ds(start, size), (row >= off) & (row < off + n))
            low = size

    def factors(source, target, i):
        def run(here, inside):
            rows = source[here, :]
            picked = jnp.where(inside, rows, jnp.zeros_like(rows))
            total = mm(cs[:, here], picked)
            target[...] = total
            filt = shapes[i] * kf[...]
            weights[half] = (filt * total[0:POINTS]).astype(BF16)
            weights[other] = (filt * total[POINTS:]).astype(BF16)
        windows(i, 128, DEPTHS, run)

    def fields(i, use):
        def run(here, inside):
            size = inside.shape[0]
            pieces = PIECES.get(size, 1)
            for n in range(pieces):
                at, step = n * (size // pieces), size // pieces
                rows = pl.ds(pl.multiple_of(here.start + at, 16), step)
                use(rows, inside[at:at + step], mm(ct[rows, :], weights[...]))
        windows(i, 16, HEIGHTS, run)

    def keep(target, here, inside, new):
        target[here, :] = jnp.where(inside, new.astype(BF16), target[here, :])

    def forward(here, inside, m):
        s = 0.5 * jnp.tanh(0.5 * m) + 0.5
        value = m * s
        keep(act, here, inside, value)
        keep(grad, here, inside, back[here, :] * (s + value * (1.0 - s)))

    @pl.loop(0, shapes.shape[0])
    def _(i):
        push, pull = pushes.at[i], pulls.at[i]
        factors(proj, push, i)
        fields(i, forward)
        factors(grad, pull, i)
        fields(i, functools.partial(keep, upd))


def reduce_kernel(
    n_dp, n_ka, mean_weights, mean_filter, act, upd, pushes, pulls, shapes, feats, cotan, w_in, w_out, kvec,
    mixed, feat_grad, grad_in, grad_out, grad_filt,
    raw, landed, gath, squares, sq_landed, sq_gath,
    s_send, s_recv, g_send, g_recv, z_send, z_recv, q_send, q_recv,
):
    me, ka = lax.axis_index("dp"), lax.axis_index("ka")
    chan = grad_in.shape[0]
    height = chan // n_dp
    barrier = pltpu.get_barrier_semaphore()

    def peer(i):
        return lax.rem(me + i, n_dp)

    @pl.loop(1, n_dp)
    def _(i):
        pl.semaphore_signal(barrier, inc=1, device_id={"dp": peer(i)}, device_id_type=MESH)

    @pl.loop(1, n_ka)
    def _(i):
        pl.semaphore_signal(barrier, inc=1, device_id={"ka": lax.rem(ka + i, n_ka)}, device_id_type=MESH)

    atoms, depth = act.shape[0], kvec.shape[1]
    raw[:, :, 0:chan] = mm_tn(act[...], cotan[...]).reshape(n_dp, height, chan).astype(BF16)
    raw[:, :, chan:2 * chan] = mm_tn(feats[...], upd[...]).reshape(n_dp, height, chan).astype(BF16)
    point = lax.broadcasted_iota(jnp.int32, (POINTS, depth), 0).astype(F32)
    hot = (point == point_of(kvec[...].astype(F32))).astype(BF16).T
    half, other = pl.ds(0, POINTS), pl.ds(POINTS, POINTS)
    rest = jnp.zeros((POINTS, chan), F32)
    for i in range(shapes.shape[0]):
        rest = rest + shapes[i] * (pushes[i, half] * pulls[i, half] + pushes[i, other] * pulls[i, other])
    own = jnp.zeros((depth, chan), F32)
    for _ in range(2):
        piece = rest.astype(BF16)
        own = own + mm(hot, piece)
        rest = rest - piece.astype(F32)
    own = jnp.concatenate([own[:, 0:chan // 2], own[:, chan // 2:]], axis=0)
    raw[:, :, 2 * chan:] = own.reshape(n_dp, height, chan // 2).astype(BF16)
    pl.semaphore_wait(barrier, n_dp - 1 + n_ka - 1)

    def scatter(i):
        return pltpu.make_async_remote_copy(
            src_ref=raw.at[peer(i)], dst_ref=landed.at[i - 1], send_sem=s_send.at[i - 1], recv_sem=s_recv.at[i - 1],
            device_id={"dp": peer(i)}, device_id_type=MESH,
        )

    def gather(i):
        return pltpu.make_async_remote_copy(
            src_ref=gath.at[me], dst_ref=gath.at[me], send_sem=g_send.at[i - 1], recv_sem=g_recv.at[i - 1],
            device_id={"dp": peer(i)}, device_id_type=MESH,
        )

    def across(i):
        return pltpu.make_async_remote_copy(
            src_ref=squares, dst_ref=sq_landed.at[i - 1], send_sem=z_send.at[i - 1], recv_sem=z_recv.at[i - 1],
            device_id={"ka": lax.rem(ka + i, n_ka)}, device_id_type=MESH,
        )

    def gather_sq(i):
        return pltpu.make_async_remote_copy(
            src_ref=sq_gath.at[me], dst_ref=sq_gath.at[me], send_sem=q_send.at[i - 1], recv_sem=q_recv.at[i - 1],
            device_id={"dp": peer(i)}, device_id_type=MESH,
        )

    def each(copy, act, n):
        @pl.loop(1, n)
        def _(i):
            act(copy(i))

    each(scatter, lambda c: c.start(), n_dp)
    for a in range(0, atoms, 512):
        mixed[a:a + 512, :] = (feats[a:a + 512, :].astype(F32) + mm(act[a:a + 512, :], w_out[...])).astype(BF16)
    each(scatter, lambda c: c.wait_recv(), n_dp)
    total = raw[me].astype(F32)
    for i in range(n_dp - 1):
        total = total + landed[i].astype(F32)
    gath[me] = total.astype(BF16)
    tail = total[:, 2 * chan:]
    squares[...] = jnp.sum(tail * tail, axis=0, keepdims=True)
    each(across, lambda c: c.start(), n_ka)
    each(gather, lambda c: c.start(), n_dp)
    for a in range(0, atoms, 512):
        feat_grad[a:a + 512, :] = (cotan[a:a + 512, :].astype(F32) + mm_nt(upd[a:a + 512, :], w_in[...])).astype(BF16)
    each(across, lambda c: c.wait_recv(), n_ka)
    added = squares[...]
    for i in range(n_ka - 1):
        added = added + sq_landed[i]
    sq_gath[me] = added
    each(gather_sq, lambda c: c.start(), n_dp)
    each(gather, lambda c: c.wait_recv(), n_dp)
    everything = gath[...].astype(F32).reshape(chan, gath.shape[2])
    weights = everything[:, 0:2 * chan]
    scale = lax.rsqrt(jnp.sum(weights * weights, axis=(0, 1), keepdims=True) * mean_weights + 1e-06)
    grad_out[...] = everything[:, 0:chan] * scale
    grad_in[...] = everything[:, chan:2 * chan] * scale
    each(gather_sq, lambda c: c.wait_recv(), n_dp)
    summed = sq_gath[...].reshape(n_dp, sq_gath.shape[2])
    scale = lax.rsqrt(jnp.sum(summed, axis=(0, 1), keepdims=True) * mean_filter + 1e-06)
    tail = everything[:, 2 * chan:] * scale
    grad_filt[...] = jnp.concatenate([tail[0:depth], tail[depth:]], axis=1)
    each(scatter, lambda c: c.wait_send(), n_dp)
    each(gather, lambda c: c.wait_send(), n_dp)
    each(across, lambda c: c.wait_send(), n_ka)
    each(gather_sq, lambda c: c.wait_send(), n_dp)


def put_kernel(*refs):
    n = (len(refs) - 1) // 2
    copies = [pltpu.make_async_copy(refs[i], refs[n + i], refs[-1].at[i]) for i in range(n)]
    for c in copies:
        c.start()
    for c in copies:
        c.wait()


def solution(mesh):
    n_dp, n_ka = mesh.shape["dp"], mesh.shape["ka"]
    vmem = pl.BlockSpec(memory_space=pltpu.VMEM)
    smem = pl.BlockSpec(memory_space=pltpu.SMEM)
    hbm = pl.BlockSpec(memory_space=pltpu.HBM)
    dma = pltpu.SemaphoreType.DMA

    def body(feats, coords, cell_ids, recip, kvec, w_in, w_out, kfilt, spread, cotan):
        atoms, chan = feats.shape
        depth = kfilt.shape[0]
        cells = recip.shape[1]
        shape = jax.ShapeDtypeStruct
        height, width = chan // n_dp, 2 * chan + depth
        part = depth // 2
        spread = spread.reshape(1, chan)

        def far(*arrays):
            return [pltpu.with_memory_space_constraint(a, pltpu.HBM) for a in arrays]

        def held(*arrays):
            return [pltpu.VMEM(a.shape, a.dtype) for a in arrays]

        cs, ct, proj, back, shapes, kf, meta = pl.pallas_call(
            functools.partial(gather_kernel, n_ka),
            out_shape=(
                shape((2 * POINTS, atoms), BF16),
                shape((atoms, 2 * POINTS), BF16),
                shape((atoms, chan), BF16),
                shape((atoms, chan), F32),
                shape((cells, POINTS, chan), F32),
                shape((POINTS, chan), F32),
                shape((1, 128), jnp.int32),
            ),
            in_specs=[hbm] * 10,
            out_specs=[vmem] * 7,
            scratch_shapes=held(feats, coords, cell_ids, recip, kvec, w_in, kfilt, spread, cotan, w_out) + [
                pltpu.VMEM((n_ka, 2, part + 8, chan), BF16),
                pltpu.VMEM((n_ka, 2, part, chan), BF16),
                dma((10,)), dma((2, 2, n_ka)), dma((2, 2, n_ka)), dma((2, 2, n_ka)), dma((2, 2, n_ka)),
            ],
            compiler_params=pltpu.CompilerParams(collective_id=0, has_side_effects=True, vmem_limit_bytes=GATHER_VMEM),
            name="gather",
        )(*far(feats, coords, cell_ids, recip, kvec, w_in, kfilt, spread, cotan, w_out))
        act, upd, pushes, pulls = pl.pallas_call(
            cell_kernel,
            out_shape=(
                shape((atoms, chan), BF16),
                shape((atoms, chan), BF16),
                shape((cells, 2 * POINTS, chan), F32),
                shape((cells, 2 * POINTS, chan), F32),
            ),
            in_specs=[smem] + [vmem] * 6,
            out_specs=[vmem] * 4,
            scratch_shapes=[pltpu.VMEM((atoms, chan), BF16), pltpu.VMEM((2 * POINTS, chan), BF16)],
            compiler_params=pltpu.CompilerParams(vmem_limit_bytes=16 << 20),
            name="cells",
        )(meta, cs, ct, proj, back, shapes, kf)
        results = pl.pallas_call(
            functools.partial(reduce_kernel, n_dp, n_ka, 1.0 / (2 * chan * chan), 1.0 / (depth * n_ka * chan)),
            out_shape=(
                shape((atoms, chan), BF16), shape((atoms, chan), BF16),
                shape((chan, chan), F32), shape((chan, chan), F32), shape((depth, chan), F32),
            ),
            in_specs=[vmem] * 10,
            out_specs=[vmem] * 5,
            scratch_shapes=[
                pltpu.VMEM((n_dp, height, width), BF16),
                pltpu.VMEM((n_dp - 1, height, width), BF16),
                pltpu.VMEM((n_dp, height, width), BF16),
                pltpu.VMEM((1, depth), F32),
                pltpu.VMEM((n_ka - 1, 1, depth), F32),
                pltpu.VMEM((n_dp, 1, depth), F32),
            ] + [dma((n_dp,))] * 4 + [dma((n_ka,))] * 2 + [dma((n_dp,))] * 2,
            compiler_params=pltpu.CompilerParams(collective_id=1, has_side_effects=True, vmem_limit_bytes=REDUCE_VMEM),
            name="reduce",
        )(act, upd, pushes, pulls, shapes, feats, cotan, w_in, w_out, kvec)
        return tuple(pl.pallas_call(
            put_kernel,
            out_shape=[shape(r.shape, r.dtype) for r in results],
            in_specs=[vmem] * 5,
            out_specs=[hbm] * 5,
            scratch_shapes=[dma((5,))],
            compiler_params=pltpu.CompilerParams(vmem_limit_bytes=16 << 20),
            name="put",
        )(*results))

    placed = (
        P("dp", None), P(None, "dp"), P("dp", None), P("dp", None, None), P(None, "ka"),
        P(), P(), P("ka", None), P(), P("dp", None),
    )
    return jax.shard_map(
        body,
        mesh=mesh,
        in_specs=placed,
        out_specs=(P("dp", None), P("dp", None), P(), P(), P("ka", None)),
        check_vma=False,
    )
```

```python
import functools

import jax
import jax.numpy as jnp
from jax import lax
from jax.experimental import pallas as pl
from jax.experimental.pallas import tpu as pltpu
from jax.sharding import PartitionSpec as P

MESH = pl.DeviceIdType.MESH
F32, BF16 = jnp.float32, jnp.bfloat16
NT = (((1,), (1,)), ((), ()))
TN = (((0,), (0,)), ((), ()))
GATHER_VMEM, REDUCE_VMEM = 30 << 20, 24 << 20
POINTS = 384
DEPTHS = (256, 512, 768, 1152)
PIECES = {544: 2, 1040: 5}
HEIGHTS = (112, 176, 240, 320, 544, 1040)
COS = (0.9999992251396179, -19.738981246948242, 64.92865753173828, -85.27162170410156, 58.79049301147461, -21.07110595703125)
SIN = (6.283185005187988, -41.341590881347656, 81.59994506835938, -76.61447143554688, 41.3428840637207, -12.471243858337402)


def poly(coefs, s):
    total = coefs[-1] * s + coefs[-2]
    for c in coefs[-3::-1]:
        total = total * s + c
    return total


def mm(a, b):
    return jnp.dot(a, b, preferred_element_type=F32)


def mm_nt(a, b):
    return lax.dot_general(a, b, NT, preferred_element_type=F32)


def mm_tn(a, b):
    return lax.dot_general(a, b, TN, preferred_element_type=F32)


def lattice(shape, axis):
    n = lax.broadcasted_iota(jnp.int32, shape, axis).astype(F32) + 364.0
    i = jnp.floor((n + 0.5) * (1.0 / 81.0))
    rest = n - 81.0 * i
    j = jnp.floor((rest + 0.5) * (1.0 / 9.0))
    return i - 4.0, j - 4.0, rest - 9.0 * j - 4.0


def point_of(k):
    return jnp.abs(81.0 * k[0:1] + 9.0 * k[1:2] + k[2:3])


def gather_kernel(
    n_ka, feats_in, coords_in, cells_in, recip_in, kvec_in, w_in_in, kfilt_in, spread_in, cotan_in, w_out_in,
    cs, ct, proj, back, shapes, kf, meta,
    feats, coords, own_cells, recip, kvec, w_in, kfilt, spread, cotan, w_out,
    high, low, loads, send, recv, p_send, p_recv,
):
    me, dp = lax.axis_index("ka"), lax.axis_index("dp")
    right, left = lax.rem(me + 1, n_ka), lax.rem(me + n_ka - 1, n_ka)
    core = lax.rem(dp, 2)
    twin = dp + 1 - 2 * core
    barrier = pltpu.get_barrier_semaphore()
    for peer in (left, right):
        pl.semaphore_signal(barrier, inc=1, device_id={"ka": peer}, device_id_type=MESH)
    pl.semaphore_signal(barrier, inc=1, device_id={"dp": twin}, device_id_type=MESH)
    pairs = (
        (kfilt_in, kfilt), (kvec_in, kvec), (coords_in, coords), (cells_in, own_cells), (w_in_in, w_in),
        (feats_in, feats), (recip_in, recip), (spread_in, spread), (w_out_in, w_out), (cotan_in, cotan),
    )
    loading = [pltpu.make_async_copy(a, b, loads.at[i]) for i, (a, b) in enumerate(pairs)]
    for c in loading:
        c.start()
    depth, chan = kfilt.shape
    part = depth // 2
    atoms = cs.shape[1]
    loading[0].wait()
    loading[1].wait()
    first = kfilt[...].astype(BF16)
    second = (kfilt[...] - first.astype(F32)).astype(BF16)
    kpad = jnp.concatenate([kvec[...].astype(F32), jnp.zeros((5, depth), F32)], axis=0)
    for h in range(2):
        rows = slice(h * part, (h + 1) * part)
        high[me, h, 0:part, :] = first[rows]
        low[me, h] = second[rows]
        k = kpad[:, rows]
        high[me, h, part:part + 8, :] = jnp.concatenate([k, k, k, k], axis=1).astype(BF16)
    pl.semaphore_wait(barrier, 3)

    hops = (n_ka // 2, n_ka - 1 - n_ka // 2)
    halves = (high, low)

    def hop(half, way, step):
        slot = lax.rem(me - step + n_ka, n_ka) if way == 0 else lax.rem(me + step, n_ka)
        ref = halves[half].at[slot, core]
        return pltpu.make_async_remote_copy(
            src_ref=ref, dst_ref=ref, send_sem=send.at[half, way, step], recv_sem=recv.at[half, way, step],
            device_id={"ka": right if way == 0 else left}, device_id_type=MESH,
        )

    def share(half, way, step):
        slot = lax.rem(me - step - 1 + n_ka, n_ka) if way == 0 else lax.rem(me + step + 1, n_ka)
        ref = halves[half].at[slot, core]
        return pltpu.make_async_remote_copy(
            src_ref=ref, dst_ref=ref, send_sem=p_send.at[half, way, step], recv_sem=p_recv.at[half, way, step],
            device_id={"dp": twin}, device_id_type=MESH,
        )

    def trig(i):
        at = pl.multiple_of(i * 16, 16)
        n = (lax.broadcasted_iota(jnp.int32, (16, 1), 0) + (at + 364)).astype(F32)
        kx = jnp.floor((n + 0.5) * (1.0 / 81.0))
        rest = n - 81.0 * kx
        ky = jnp.floor((rest + 0.5) * (1.0 / 9.0))
        kz = rest - 9.0 * ky - 4.0
        kx, ky = kx - 4.0, ky - 4.0
        for lane in range(0, atoms, 512):
            here = pl.ds(lane, 512)
            turn = (coords[0:1, here] * kx + coords[1:2, here] * ky) + coords[2:3, here] * kz
            turn = turn - jnp.round(turn)
            s = turn * turn
            cs[pl.ds(at, 16), here] = poly(COS, s).astype(BF16)
            cs[pl.ds(POINTS + at, 16), here] = (turn * poly(SIN, s)).astype(BF16)

    chunks = POINTS // 16

    def envelope():
        loading[3].wait()
        loading[6].wait()
        loading[7].wait()
        n_cells = recip.shape[1]
        own = own_cells[...]
        lane = lax.broadcasted_iota(jnp.int32, (1, 128), 1)
        info = jnp.zeros((1, 128), jnp.int32)
        kx, ky, kz = lattice((1, POINTS), 1)
        b = recip[0]
        q = jnp.zeros((n_cells, POINTS), F32)
        for r in range(3):
            dot = (b[:, 3 * r:3 * r + 1] * kx + b[:, 3 * r + 1:3 * r + 2] * ky) + b[:, 3 * r + 2:3 * r + 3] * kz
            q = q + dot * dot
        q = jnp.concatenate([q] + [jnp.zeros((128 - n_cells, POINTS), F32)], axis=0).T
        for i in range(n_cells):
            count = jnp.sum((own == i).astype(F32), axis=1, keepdims=True)
            before = jnp.sum((own < i).astype(F32), axis=1, keepdims=True)
            info = jnp.where(lane == i, before.astype(jnp.int32), info)
            info = jnp.where(lane == 8 + i, count.astype(jnp.int32), info)
            shapes[i] = jnp.exp(-(q[:, i:i + 1] * spread[...])) * (1.0 / count)
        meta[...] = info

    pending, shared = [], []

    def ways(step):
        return [way for way in (0, 1) if 0 <= step < hops[way]]

    def slots_of(step):
        return [lax.rem(me + n_ka - step - 1, n_ka) if way == 0 else lax.rem(me + step + 1, n_ka) for way in ways(step)]

    def arrived(step):
        for half in (0, 1):
            for way in ways(step - 1):
                share(half, way, step - 1).wait_recv()

    def filter_of(slots, begin=False):
        point = lax.broadcasted_iota(jnp.int32, (POINTS, 2 * depth), 0).astype(F32)
        total = None
        for z in slots:
            k = jnp.concatenate([high[z, h, part:part + 8, 0:depth] for h in (0, 1)], axis=1).astype(F32)
            hot = (point == point_of(k)).astype(BF16)
            terms = jnp.concatenate([high[z, 0, 0:part, :], low[z, 0], high[z, 1, 0:part, :], low[z, 1]], axis=0)
            new = mm(hot, terms)
            total = new if total is None else total + new
        if begin:
            kf[...] = total
        else:
            kf[...] += total

    def stage(step):
        if step == 0:
            loading[4].wait()
            loading[5].wait()
            proj[...] = mm(feats[...], w_in[...]).astype(BF16)
            loading[2].wait()
            pl.loop(0, 10)(trig)
        elif step == 1:
            filter_of([me], True)
            pl.loop(10, 21)(trig)
        elif step == 2:
            pl.loop(21, chunks)(trig)
            envelope()
            loading[8].wait()
            loading[9].wait()
            back[...] = mm_nt(cotan[...], w_out[...])
        else:
            arrived(1)
            filter_of(slots_of(0))
            for p in range(0, 2 * POINTS, 256):
                for a in range(0, atoms, 256):
                    ct[a:a + 256, p:p + 256] = cs[p:p + 256, a:a + 256].T
            arrived(2)
            filter_of(slots_of(1))


    for step in range(hops[0] + 1):
        for half in (0, 1):
            for way in ways(step - 1):
                hop(half, way, step - 1).wait_recv()
            for way in ways(step):
                c = hop(half, way, step)
                c.start()
                pending.append(c)
            for way in ways(step - 1):
                c = share(half, way, step - 1)
                c.start()
                shared.append(c)
        if step < hops[0]:
            stage(step)
    for step in (3, 4):
        arrived(step)
        filter_of(slots_of(step - 1))
    for c in pending + shared:
        c.wait_send()


def cell_kernel(meta, cs, ct, proj, back, shapes, kf, act, upd, rsum, grad, weights, push):
    atoms = cs.shape[1]
    half, other = pl.ds(0, POINTS), pl.ds(POINTS, POINTS)

    def windows(i, unit, sizes, run):
        off, n = meta[0, i], meta[0, 8 + i]
        base = lax.div(off, unit) * unit
        span = off + n - base
        low = 0
        for size in sizes:
            @pl.when((span > low) & (span <= size))
            def _():
                start = pl.multiple_of(jnp.minimum(base, atoms - size), unit)
                row = lax.broadcasted_iota(jnp.int32, (size, 1), 0) + start
                run(pl.ds(start, size), (row >= off) & (row < off + n))
            low = size

    def factors(source, i, use):
        def run(here, inside):
            rows = source[here, :]
            picked = jnp.where(inside, rows, jnp.zeros_like(rows))
            total = mm(cs[:, here], picked)
            shape = shapes[i]
            use(shape, total)
            filt = shape * kf[...]
            weights[half] = (filt * total[0:POINTS]).astype(BF16)
            weights[other] = (filt * total[POINTS:]).astype(BF16)
        windows(i, 128, DEPTHS, run)

    def fields(i, use):
        def run(here, inside):
            size = inside.shape[0]
            pieces = PIECES.get(size, 1)
            for n in range(pieces):
                at, step = n * (size // pieces), size // pieces
                rows = pl.ds(pl.multiple_of(here.start + at, 16), step)
                use(rows, inside[at:at + step], mm(ct[rows, :], weights[...]))
        windows(i, 16, HEIGHTS, run)

    def keep(target, here, inside, new):
        target[here, :] = jnp.where(inside, new.astype(BF16), target[here, :])

    def forward(here, inside, m):
        s = 0.5 * jnp.tanh(0.5 * m) + 0.5
        value = m * s
        keep(act, here, inside, value)
        keep(grad, here, inside, back[here, :] * (s + value * (1.0 - s)))

    def hold(shape, total):
        push[...] = total

    def add(shape, total):
        rsum[...] += shape * (push[half] * total[0:POINTS] + push[other] * total[POINTS:])

    rsum[...] = jnp.zeros_like(rsum)

    @pl.loop(0, shapes.shape[0])
    def _(i):
        factors(proj, i, hold)
        fields(i, forward)
        factors(grad, i, add)
        fields(i, functools.partial(keep, upd))


def reduce_kernel(
    n_dp, n_ka, mean_weights, mean_filter, act, upd, rsum, feats, cotan, w_in, w_out, kvec,
    mixed, feat_grad, grad_in, grad_out, grad_filt,
    raw, landed, gath, squares, sq_landed, sq_gath,
    s_send, s_recv, g_send, g_recv, z_send, z_recv, q_send, q_recv,
):
    me, ka = lax.axis_index("dp"), lax.axis_index("ka")
    chan = grad_in.shape[0]
    height = chan // n_dp
    barrier = pltpu.get_barrier_semaphore()

    def peer(i):
        return lax.rem(me + i, n_dp)

    @pl.loop(1, n_dp)
    def _(i):
        pl.semaphore_signal(barrier, inc=1, device_id={"dp": peer(i)}, device_id_type=MESH)

    @pl.loop(1, n_ka)
    def _(i):
        pl.semaphore_signal(barrier, inc=1, device_id={"ka": lax.rem(ka + i, n_ka)}, device_id_type=MESH)

    atoms, depth = act.shape[0], kvec.shape[1]
    raw[:, :, 0:chan] = mm_tn(act[...], cotan[...]).reshape(n_dp, height, chan).astype(BF16)
    raw[:, :, chan:2 * chan] = mm_tn(feats[...], upd[...]).reshape(n_dp, height, chan).astype(BF16)
    point = lax.broadcasted_iota(jnp.int32, (POINTS, depth), 0).astype(F32)
    hot = (point == point_of(kvec[...].astype(F32))).astype(BF16).T
    rest = rsum[...]
    own = jnp.zeros((depth, chan), F32)
    for _ in range(2):
        piece = rest.astype(BF16)
        own = own + mm(hot, piece)
        rest = rest - piece.astype(F32)
    own = jnp.concatenate([own[:, 0:chan // 2], own[:, chan // 2:]], axis=0)
    raw[:, :, 2 * chan:] = own.reshape(n_dp, height, chan // 2).astype(BF16)
    pl.semaphore_wait(barrier, n_dp - 1 + n_ka - 1)

    def scatter(i):
        return pltpu.make_async_remote_copy(
            src_ref=raw.at[peer(i)], dst_ref=landed.at[i - 1], send_sem=s_send.at[i - 1], recv_sem=s_recv.at[i - 1],
            device_id={"dp": peer(i)}, device_id_type=MESH,
        )

    def gather(i):
        return pltpu.make_async_remote_copy(
            src_ref=gath.at[me], dst_ref=gath.at[me], send_sem=g_send.at[i - 1], recv_sem=g_recv.at[i - 1],
            device_id={"dp": peer(i)}, device_id_type=MESH,
        )

    def across(i):
        return pltpu.make_async_remote_copy(
            src_ref=squares, dst_ref=sq_landed.at[i - 1], send_sem=z_send.at[i - 1], recv_sem=z_recv.at[i - 1],
            device_id={"ka": lax.rem(ka + i, n_ka)}, device_id_type=MESH,
        )

    def gather_sq(i):
        return pltpu.make_async_remote_copy(
            src_ref=sq_gath.at[me], dst_ref=sq_gath.at[me], send_sem=q_send.at[i - 1], recv_sem=q_recv.at[i - 1],
            device_id={"dp": peer(i)}, device_id_type=MESH,
        )

    def each(copy, act, n):
        @pl.loop(1, n)
        def _(i):
            act(copy(i))

    each(scatter, lambda c: c.start(), n_dp)
    for a in range(0, atoms, 512):
        mixed[a:a + 512, :] = (feats[a:a + 512, :].astype(F32) + mm(act[a:a + 512, :], w_out[...])).astype(BF16)
    each(scatter, lambda c: c.wait_recv(), n_dp)
    total = raw[me].astype(F32)
    for i in range(n_dp - 1):
        total = total + landed[i].astype(F32)
    gath[me] = total.astype(BF16)
    tail = total[:, 2 * chan:]
    squares[...] = jnp.sum(tail * tail, axis=0, keepdims=True)
    each(across, lambda c: c.start(), n_ka)
    each(gather, lambda c: c.start(), n_dp)
    for a in range(0, atoms, 512):
        feat_grad[a:a + 512, :] = (cotan[a:a + 512, :].astype(F32) + mm_nt(upd[a:a + 512, :], w_in[...])).astype(BF16)
    each(across, lambda c: c.wait_recv(), n_ka)
    added = squares[...]
    for i in range(n_ka - 1):
        added = added + sq_landed[i]
    sq_gath[me] = added
    each(gather_sq, lambda c: c.start(), n_dp)
    each(gather, lambda c: c.wait_recv(), n_dp)
    everything = gath[...].astype(F32).reshape(chan, gath.shape[2])
    weights = everything[:, 0:2 * chan]
    scale = lax.rsqrt(jnp.sum(weights * weights, axis=(0, 1), keepdims=True) * mean_weights + 1e-06)
    grad_out[...] = everything[:, 0:chan] * scale
    grad_in[...] = everything[:, chan:2 * chan] * scale
    each(gather_sq, lambda c: c.wait_recv(), n_dp)
    summed = sq_gath[...].reshape(n_dp, sq_gath.shape[2])
    scale = lax.rsqrt(jnp.sum(summed, axis=(0, 1), keepdims=True) * mean_filter + 1e-06)
    tail = everything[:, 2 * chan:] * scale
    grad_filt[...] = jnp.concatenate([tail[0:depth], tail[depth:]], axis=1)
    each(scatter, lambda c: c.wait_send(), n_dp)
    each(gather, lambda c: c.wait_send(), n_dp)
    each(across, lambda c: c.wait_send(), n_ka)
    each(gather_sq, lambda c: c.wait_send(), n_dp)


def put_kernel(*refs):
    n = (len(refs) - 1) // 2
    copies = [pltpu.make_async_copy(refs[i], refs[n + i], refs[-1].at[i]) for i in range(n)]
    for c in copies:
        c.start()
    for c in copies:
        c.wait()


def solution(mesh):
    n_dp, n_ka = mesh.shape["dp"], mesh.shape["ka"]
    vmem = pl.BlockSpec(memory_space=pltpu.VMEM)
    smem = pl.BlockSpec(memory_space=pltpu.SMEM)
    hbm = pl.BlockSpec(memory_space=pltpu.HBM)
    dma = pltpu.SemaphoreType.DMA

    def body(feats, coords, cell_ids, recip, kvec, w_in, w_out, kfilt, spread, cotan):
        atoms, chan = feats.shape
        depth = kfilt.shape[0]
        cells = recip.shape[1]
        shape = jax.ShapeDtypeStruct
        height, width = chan // n_dp, 2 * chan + depth
        part = depth // 2
        spread = spread.reshape(1, chan)

        def far(*arrays):
            return [pltpu.with_memory_space_constraint(a, pltpu.HBM) for a in arrays]

        def held(*arrays):
            return [pltpu.VMEM(a.shape, a.dtype) for a in arrays]

        cs, ct, proj, back, shapes, kf, meta = pl.pallas_call(
            functools.partial(gather_kernel, n_ka),
            out_shape=(
                shape((2 * POINTS, atoms), BF16),
                shape((atoms, 2 * POINTS), BF16),
                shape((atoms, chan), BF16),
                shape((atoms, chan), F32),
                shape((cells, POINTS, chan), F32),
                shape((POINTS, chan), F32),
                shape((1, 128), jnp.int32),
            ),
            in_specs=[hbm] * 10,
            out_specs=[vmem] * 7,
            scratch_shapes=held(feats, coords, cell_ids, recip, kvec, w_in, kfilt, spread, cotan, w_out) + [
                pltpu.VMEM((n_ka, 2, part + 8, chan), BF16),
                pltpu.VMEM((n_ka, 2, part, chan), BF16),
                dma((10,)), dma((2, 2, n_ka)), dma((2, 2, n_ka)), dma((2, 2, n_ka)), dma((2, 2, n_ka)),
            ],
            compiler_params=pltpu.CompilerParams(collective_id=0, has_side_effects=True, vmem_limit_bytes=GATHER_VMEM),
            name="gather",
        )(*far(feats, coords, cell_ids, recip, kvec, w_in, kfilt, spread, cotan, w_out))
        act, upd, rsum = pl.pallas_call(
            cell_kernel,
            out_shape=(
                shape((atoms, chan), BF16),
                shape((atoms, chan), BF16),
                shape((POINTS, chan), F32),
            ),
            in_specs=[smem] + [vmem] * 6,
            out_specs=[vmem] * 3,
            scratch_shapes=[
                pltpu.VMEM((atoms, chan), BF16),
                pltpu.VMEM((2 * POINTS, chan), BF16),
                pltpu.VMEM((2 * POINTS, chan), F32),
            ],
            compiler_params=pltpu.CompilerParams(vmem_limit_bytes=16 << 20),
            name="cells",
        )(meta, cs, ct, proj, back, shapes, kf)
        results = pl.pallas_call(
            functools.partial(reduce_kernel, n_dp, n_ka, 1.0 / (2 * chan * chan), 1.0 / (depth * n_ka * chan)),
            out_shape=(
                shape((atoms, chan), BF16), shape((atoms, chan), BF16),
                shape((chan, chan), F32), shape((chan, chan), F32), shape((depth, chan), F32),
            ),
            in_specs=[vmem] * 8,
            out_specs=[vmem] * 5,
            scratch_shapes=[
                pltpu.VMEM((n_dp, height, width), BF16),
                pltpu.VMEM((n_dp - 1, height, width), BF16),
                pltpu.VMEM((n_dp, height, width), BF16),
                pltpu.VMEM((1, depth), F32),
                pltpu.VMEM((n_ka - 1, 1, depth), F32),
                pltpu.VMEM((n_dp, 1, depth), F32),
            ] + [dma((n_dp,))] * 4 + [dma((n_ka,))] * 2 + [dma((n_dp,))] * 2,
            compiler_params=pltpu.CompilerParams(collective_id=1, has_side_effects=True, vmem_limit_bytes=REDUCE_VMEM),
            name="reduce",
        )(act, upd, rsum, feats, cotan, w_in, w_out, kvec)
        return tuple(pl.pallas_call(
            put_kernel,
            out_shape=[shape(r.shape, r.dtype) for r in results],
            in_specs=[vmem] * 5,
            out_specs=[hbm] * 5,
            scratch_shapes=[dma((5,))],
            compiler_params=pltpu.CompilerParams(vmem_limit_bytes=16 << 20),
            name="put",
        )(*results))

    placed = (
        P("dp", None), P(None, "dp"), P("dp", None), P("dp", None, None), P(None, "ka"),
        P(), P(), P("ka", None), P(), P("dp", None),
    )
    return jax.shard_map(
        body,
        mesh=mesh,
        in_specs=placed,
        out_specs=(P("dp", None), P("dp", None), P(), P(), P("ka", None)),
        check_vma=False,
    )
```

```python
import functools

import jax
import jax.numpy as jnp
from jax import lax
from jax.experimental import pallas as pl
from jax.experimental.pallas import tpu as pltpu
from jax.sharding import PartitionSpec as P

MESH = pl.DeviceIdType.MESH
F32, BF16 = jnp.float32, jnp.bfloat16
NT = (((1,), (1,)), ((), ()))
TN = (((0,), (0,)), ((), ()))
GATHER_VMEM, REDUCE_VMEM = 30 << 20, 24 << 20
POINTS = 384
DEPTHS = (256, 512, 768, 1152)
PIECES = {544: 2, 1040: 5}
HEIGHTS = (112, 176, 240, 320, 544, 1040)
COS = (0.9999992251396179, -19.738981246948242, 64.92865753173828, -85.27162170410156, 58.79049301147461, -21.07110595703125)
SIN = (6.283185005187988, -41.341590881347656, 81.59994506835938, -76.61447143554688, 41.3428840637207, -12.471243858337402)


def poly(coefs, s):
    total = coefs[-1] * s + coefs[-2]
    for c in coefs[-3::-1]:
        total = total * s + c
    return total


def mm(a, b):
    return jnp.dot(a, b, preferred_element_type=F32)


def mm_nt(a, b):
    return lax.dot_general(a, b, NT, preferred_element_type=F32)


def mm_tn(a, b):
    return lax.dot_general(a, b, TN, preferred_element_type=F32)


def lattice(shape, axis):
    n = lax.broadcasted_iota(jnp.int32, shape, axis).astype(F32) + 364.0
    i = jnp.floor((n + 0.5) * (1.0 / 81.0))
    rest = n - 81.0 * i
    j = jnp.floor((rest + 0.5) * (1.0 / 9.0))
    return i - 4.0, j - 4.0, rest - 9.0 * j - 4.0


def point_of(k):
    return jnp.abs(81.0 * k[0:1] + 9.0 * k[1:2] + k[2:3])


def gather_kernel(
    n_ka, feats_in, coords_in, cells_in, recip_in, kvec_in, w_in_in, kfilt_in, spread_in, cotan_in, w_out_in,
    cs, ct, proj, back, shapes, kf, meta,
    feats, coords, own_cells, recip, kvec, w_in, kfilt, spread, cotan, w_out,
    high, low, loads, send, recv, p_send, p_recv,
):
    me, dp = lax.axis_index("ka"), lax.axis_index("dp")
    right, left = lax.rem(me + 1, n_ka), lax.rem(me + n_ka - 1, n_ka)
    core = lax.rem(dp, 2)
    twin = dp + 1 - 2 * core
    barrier = pltpu.get_barrier_semaphore()
    for peer in (left, right):
        pl.semaphore_signal(barrier, inc=1, device_id={"ka": peer}, device_id_type=MESH)
    pl.semaphore_signal(barrier, inc=1, device_id={"dp": twin}, device_id_type=MESH)
    pairs = (
        (kfilt_in, kfilt), (kvec_in, kvec), (coords_in, coords), (cells_in, own_cells), (w_in_in, w_in),
        (feats_in, feats), (recip_in, recip), (spread_in, spread), (w_out_in, w_out), (cotan_in, cotan),
    )
    loading = [pltpu.make_async_copy(a, b, loads.at[i]) for i, (a, b) in enumerate(pairs)]
    for c in loading:
        c.start()
    depth, chan = kfilt.shape
    part = depth // 2
    atoms = cs.shape[1]
    loading[0].wait()
    loading[1].wait()
    first = kfilt[...].astype(BF16)
    second = (kfilt[...] - first.astype(F32)).astype(BF16)
    kpad = jnp.concatenate([kvec[...].astype(F32), jnp.zeros((5, depth), F32)], axis=0)
    for h in range(2):
        rows = slice(h * part, (h + 1) * part)
        high[me, h, 0:part, :] = first[rows]
        low[me, h] = second[rows]
        k = kpad[:, rows]
        high[me, h, part:part + 8, :] = jnp.concatenate([k, k, k, k], axis=1).astype(BF16)
    pl.semaphore_wait(barrier, 3)

    hops = (n_ka // 2, n_ka - 1 - n_ka // 2)
    halves = (high, low)

    def hop(half, way, step):
        slot = lax.rem(me - step + n_ka, n_ka) if way == 0 else lax.rem(me + step, n_ka)
        ref = halves[half].at[slot, core]
        return pltpu.make_async_remote_copy(
            src_ref=ref, dst_ref=ref, send_sem=send.at[half, way, step], recv_sem=recv.at[half, way, step],
            device_id={"ka": right if way == 0 else left}, device_id_type=MESH,
        )

    def share(half, way, step):
        slot = lax.rem(me - step - 1 + n_ka, n_ka) if way == 0 else lax.rem(me + step + 1, n_ka)
        ref = halves[half].at[slot, core]
        return pltpu.make_async_remote_copy(
            src_ref=ref, dst_ref=ref, send_sem=p_send.at[half, way, step], recv_sem=p_recv.at[half, way, step],
            device_id={"dp": twin}, device_id_type=MESH,
        )

    def trig(i):
        at = pl.multiple_of(i * 16, 16)
        n = (lax.broadcasted_iota(jnp.int32, (16, 1), 0) + (at + 364)).astype(F32)
        kx = jnp.floor((n + 0.5) * (1.0 / 81.0))
        rest = n - 81.0 * kx
        ky = jnp.floor((rest + 0.5) * (1.0 / 9.0))
        kz = rest - 9.0 * ky - 4.0
        kx, ky = kx - 4.0, ky - 4.0
        for lane in range(0, atoms, 512):
            here = pl.ds(lane, 512)
            turn = (coords[0:1, here] * kx + coords[1:2, here] * ky) + coords[2:3, here] * kz
            turn = turn - jnp.round(turn)
            s = turn * turn
            cs[pl.ds(at, 16), here] = poly(COS, s).astype(BF16)
            cs[pl.ds(POINTS + at, 16), here] = (turn * poly(SIN, s)).astype(BF16)

    chunks = POINTS // 16

    def envelope():
        loading[3].wait()
        loading[6].wait()
        loading[7].wait()
        n_cells = recip.shape[1]
        own = own_cells[...]
        lane = lax.broadcasted_iota(jnp.int32, (1, 128), 1)
        info = jnp.zeros((1, 128), jnp.int32)
        kx, ky, kz = lattice((1, POINTS), 1)
        b = recip[0]
        q = jnp.zeros((n_cells, POINTS), F32)
        for r in range(3):
            dot = (b[:, 3 * r:3 * r + 1] * kx + b[:, 3 * r + 1:3 * r + 2] * ky) + b[:, 3 * r + 2:3 * r + 3] * kz
            q = q + dot * dot
        q = jnp.concatenate([q] + [jnp.zeros((128 - n_cells, POINTS), F32)], axis=0).T
        for i in range(n_cells):
            count = jnp.sum((own == i).astype(F32), axis=1, keepdims=True)
            before = jnp.sum((own < i).astype(F32), axis=1, keepdims=True)
            info = jnp.where(lane == i, before.astype(jnp.int32), info)
            info = jnp.where(lane == 8 + i, count.astype(jnp.int32), info)
            shapes[i] = jnp.exp(-(q[:, i:i + 1] * spread[...])) * (1.0 / count)
        meta[...] = info

    pending, shared = [], []

    def ways(step):
        return [way for way in (0, 1) if 0 <= step < hops[way]]

    def slots_of(step):
        return [lax.rem(me + n_ka - step - 1, n_ka) if way == 0 else lax.rem(me + step + 1, n_ka) for way in ways(step)]

    def arrived(step):
        for half in (0, 1):
            for way in ways(step - 1):
                share(half, way, step - 1).wait_recv()

    def filter_of(slots, begin=False):
        point = lax.broadcasted_iota(jnp.int32, (POINTS, 2 * depth), 0).astype(F32)
        total = None
        for z in slots:
            k = jnp.concatenate([high[z, h, part:part + 8, 0:depth] for h in (0, 1)], axis=1).astype(F32)
            hot = (point == point_of(k)).astype(BF16)
            terms = jnp.concatenate([high[z, 0, 0:part, :], low[z, 0], high[z, 1, 0:part, :], low[z, 1]], axis=0)
            new = mm(hot, terms)
            total = new if total is None else total + new
        if begin:
            kf[...] = total
        else:
            kf[...] += total

    def stage(step):
        if step == 0:
            loading[4].wait()
            loading[5].wait()
            proj[...] = mm(feats[...], w_in[...]).astype(BF16)
            loading[2].wait()
            pl.loop(0, 10)(trig)
        elif step == 1:
            filter_of([me], True)
            pl.loop(10, 21)(trig)
        elif step == 2:
            pl.loop(21, chunks)(trig)
            envelope()
            loading[8].wait()
            loading[9].wait()
            back[...] = mm_nt(cotan[...], w_out[...])
        else:
            arrived(1)
            filter_of(slots_of(0))
            for p in range(0, 2 * POINTS, 256):
                for a in range(0, atoms, 256):
                    ct[a:a + 256, p:p + 256] = cs[p:p + 256, a:a + 256].T
            arrived(2)
            filter_of(slots_of(1))


    for step in range(hops[0] + 1):
        for half in (0, 1):
            for way in ways(step - 1):
                hop(half, way, step - 1).wait_recv()
            for way in ways(step):
                c = hop(half, way, step)
                c.start()
                pending.append(c)
            for way in ways(step - 1):
                c = share(half, way, step - 1)
                c.start()
                shared.append(c)
        if step < hops[0]:
            stage(step)
    for step in (3, 4):
        arrived(step)
        filter_of(slots_of(step - 1))
    for c in pending + shared:
        c.wait_send()


def cell_kernel(meta, cs, ct, proj, back, shapes, kf, act, upd, rsum, grad, weights, push):
    atoms = cs.shape[1]
    half, other = pl.ds(0, POINTS), pl.ds(POINTS, POINTS)

    def windows(i, unit, sizes, run):
        off, n = meta[0, i], meta[0, 8 + i]
        base = lax.div(off, unit) * unit
        span = off + n - base
        low = 0
        for size in sizes:
            @pl.when((span > low) & (span <= size))
            def _():
                start = pl.multiple_of(jnp.minimum(base, atoms - size), unit)
                row = lax.broadcasted_iota(jnp.int32, (size, 1), 0) + start
                run(pl.ds(start, size), (row >= off) & (row < off + n))
            low = size

    def factors(source, i, use):
        def run(here, inside):
            rows = source[here, :]
            picked = jnp.where(inside, rows, jnp.zeros_like(rows))
            total = mm(cs[:, here], picked)
            shape = shapes[i]
            use(shape, total)
            filt = shape * kf[...]
            weights[half] = (filt * total[0:POINTS]).astype(BF16)
            weights[other] = (filt * total[POINTS:]).astype(BF16)
        windows(i, 128, DEPTHS, run)

    def fields(i, use):
        def run(here, inside):
            size = inside.shape[0]
            pieces = PIECES.get(size, 1)
            for n in range(pieces):
                at, step = n * (size // pieces), size // pieces
                rows = pl.ds(pl.multiple_of(here.start + at, 16), step)
                use(rows, inside[at:at + step], mm(ct[rows, :], weights[...]))
        windows(i, 16, HEIGHTS, run)

    def keep(target, here, inside, new):
        target[here, :] = jnp.where(inside, new.astype(BF16), target[here, :])

    def forward(here, inside, m):
        s = 0.5 * jnp.tanh(0.5 * m) + 0.5
        value = m * s
        keep(act, here, inside, value)
        keep(grad, here, inside, back[here, :] * (s + value * (1.0 - s)))

    def hold(shape, total):
        push[...] = total

    def add(shape, total):
        rsum[...] += shape * (push[half] * total[0:POINTS] + push[other] * total[POINTS:])

    rsum[...] = jnp.zeros_like(rsum)

    @pl.loop(0, shapes.shape[0])
    def _(i):
        factors(proj, i, hold)
        fields(i, forward)
        factors(grad, i, add)
        fields(i, functools.partial(keep, upd))


def reduce_kernel(
    n_dp, n_ka, mean_weights, mean_filter, act, upd, rsum, feats, cotan, w_in, w_out, kvec,
    mixed, feat_grad, grad_in, grad_out, grad_filt,
    raw, landed, gath, squares, sq_landed, sq_gath,
    s_send, s_recv, g_send, g_recv, z_send, z_recv, q_send, q_recv,
):
    me, ka = lax.axis_index("dp"), lax.axis_index("ka")
    chan = grad_in.shape[0]
    height = chan // n_dp
    barrier = pltpu.get_barrier_semaphore()

    def peer(i):
        return lax.rem(me + i, n_dp)

    @pl.loop(1, n_dp)
    def _(i):
        pl.semaphore_signal(barrier, inc=1, device_id={"dp": peer(i)}, device_id_type=MESH)

    @pl.loop(1, n_ka)
    def _(i):
        pl.semaphore_signal(barrier, inc=1, device_id={"ka": lax.rem(ka + i, n_ka)}, device_id_type=MESH)

    atoms, depth = act.shape[0], kvec.shape[1]
    raw[:, :, 0:chan] = mm_tn(act[...], cotan[...]).reshape(n_dp, height, chan).astype(BF16)
    raw[:, :, chan:2 * chan] = mm_tn(feats[...], upd[...]).reshape(n_dp, height, chan).astype(BF16)
    point = lax.broadcasted_iota(jnp.int32, (POINTS, depth), 0).astype(F32)
    hot = (point == point_of(kvec[...].astype(F32))).astype(BF16).T
    rest = rsum[...]
    own = jnp.zeros((depth, chan), F32)
    for _ in range(2):
        piece = rest.astype(BF16)
        own = own + mm(hot, piece)
        rest = rest - piece.astype(F32)
    own = jnp.concatenate([own[:, 0:chan // 2], own[:, chan // 2:]], axis=0)
    raw[:, :, 2 * chan:] = own.reshape(n_dp, height, chan // 2).astype(BF16)
    pl.semaphore_wait(barrier, n_dp - 1 + n_ka - 1)

    def scatter(i):
        return pltpu.make_async_remote_copy(
            src_ref=raw.at[peer(i)], dst_ref=landed.at[i - 1], send_sem=s_send.at[i - 1], recv_sem=s_recv.at[i - 1],
            device_id={"dp": peer(i)}, device_id_type=MESH,
        )

    def gather(i):
        return pltpu.make_async_remote_copy(
            src_ref=gath.at[me], dst_ref=gath.at[me], send_sem=g_send.at[i - 1], recv_sem=g_recv.at[i - 1],
            device_id={"dp": peer(i)}, device_id_type=MESH,
        )

    def across(i):
        return pltpu.make_async_remote_copy(
            src_ref=squares, dst_ref=sq_landed.at[i - 1], send_sem=z_send.at[i - 1], recv_sem=z_recv.at[i - 1],
            device_id={"ka": lax.rem(ka + i, n_ka)}, device_id_type=MESH,
        )

    def gather_sq(i):
        return pltpu.make_async_remote_copy(
            src_ref=sq_gath.at[me], dst_ref=sq_gath.at[me], send_sem=q_send.at[i - 1], recv_sem=q_recv.at[i - 1],
            device_id={"dp": peer(i)}, device_id_type=MESH,
        )

    def each(copy, act, n):
        @pl.loop(1, n)
        def _(i):
            act(copy(i))

    for i in range(1, n_dp):
        scatter(i).start()
    for a in range(0, atoms, 512):
        mixed[a:a + 512, :] = (feats[a:a + 512, :].astype(F32) + mm(act[a:a + 512, :], w_out[...])).astype(BF16)
    each(scatter, lambda c: c.wait_recv(), n_dp)
    total = raw[me].astype(F32)
    for i in range(n_dp - 1):
        total = total + landed[i].astype(F32)
    gath[me] = total.astype(BF16)
    tail = total[:, 2 * chan:]
    squares[...] = jnp.sum(tail * tail, axis=0, keepdims=True)
    each(across, lambda c: c.start(), n_ka)
    for i in range(1, n_dp):
        gather(i).start()
    for a in range(0, atoms, 512):
        feat_grad[a:a + 512, :] = (cotan[a:a + 512, :].astype(F32) + mm_nt(upd[a:a + 512, :], w_in[...])).astype(BF16)
    each(across, lambda c: c.wait_recv(), n_ka)
    added = squares[...]
    for i in range(n_ka - 1):
        added = added + sq_landed[i]
    sq_gath[me] = added
    each(gather_sq, lambda c: c.start(), n_dp)
    each(gather, lambda c: c.wait_recv(), n_dp)
    everything = gath[...].astype(F32).reshape(chan, gath.shape[2])
    weights = everything[:, 0:2 * chan]
    scale = lax.rsqrt(jnp.sum(weights * weights, axis=(0, 1), keepdims=True) * mean_weights + 1e-06)
    grad_out[...] = everything[:, 0:chan] * scale
    grad_in[...] = everything[:, chan:2 * chan] * scale
    each(gather_sq, lambda c: c.wait_recv(), n_dp)
    summed = sq_gath[...].reshape(n_dp, sq_gath.shape[2])
    scale = lax.rsqrt(jnp.sum(summed, axis=(0, 1), keepdims=True) * mean_filter + 1e-06)
    tail = everything[:, 2 * chan:] * scale
    grad_filt[...] = jnp.concatenate([tail[0:depth], tail[depth:]], axis=1)
    each(scatter, lambda c: c.wait_send(), n_dp)
    each(gather, lambda c: c.wait_send(), n_dp)
    each(across, lambda c: c.wait_send(), n_ka)
    each(gather_sq, lambda c: c.wait_send(), n_dp)


def put_kernel(*refs):
    n = (len(refs) - 1) // 2
    copies = [pltpu.make_async_copy(refs[i], refs[n + i], refs[-1].at[i]) for i in range(n)]
    for c in copies:
        c.start()
    for c in copies:
        c.wait()


def solution(mesh):
    n_dp, n_ka = mesh.shape["dp"], mesh.shape["ka"]
    vmem = pl.BlockSpec(memory_space=pltpu.VMEM)
    smem = pl.BlockSpec(memory_space=pltpu.SMEM)
    hbm = pl.BlockSpec(memory_space=pltpu.HBM)
    dma = pltpu.SemaphoreType.DMA

    def body(feats, coords, cell_ids, recip, kvec, w_in, w_out, kfilt, spread, cotan):
        atoms, chan = feats.shape
        depth = kfilt.shape[0]
        cells = recip.shape[1]
        shape = jax.ShapeDtypeStruct
        height, width = chan // n_dp, 2 * chan + depth
        part = depth // 2
        spread = spread.reshape(1, chan)

        def far(*arrays):
            return [pltpu.with_memory_space_constraint(a, pltpu.HBM) for a in arrays]

        def held(*arrays):
            return [pltpu.VMEM(a.shape, a.dtype) for a in arrays]

        cs, ct, proj, back, shapes, kf, meta = pl.pallas_call(
            functools.partial(gather_kernel, n_ka),
            out_shape=(
                shape((2 * POINTS, atoms), BF16),
                shape((atoms, 2 * POINTS), BF16),
                shape((atoms, chan), BF16),
                shape((atoms, chan), F32),
                shape((cells, POINTS, chan), F32),
                shape((POINTS, chan), F32),
                shape((1, 128), jnp.int32),
            ),
            in_specs=[hbm] * 10,
            out_specs=[vmem] * 7,
            scratch_shapes=held(feats, coords, cell_ids, recip, kvec, w_in, kfilt, spread, cotan, w_out) + [
                pltpu.VMEM((n_ka, 2, part + 8, chan), BF16),
                pltpu.VMEM((n_ka, 2, part, chan), BF16),
                dma((10,)), dma((2, 2, n_ka)), dma((2, 2, n_ka)), dma((2, 2, n_ka)), dma((2, 2, n_ka)),
            ],
            compiler_params=pltpu.CompilerParams(collective_id=0, has_side_effects=True, vmem_limit_bytes=GATHER_VMEM),
            name="gather",
        )(*far(feats, coords, cell_ids, recip, kvec, w_in, kfilt, spread, cotan, w_out))
        act, upd, rsum = pl.pallas_call(
            cell_kernel,
            out_shape=(
                shape((atoms, chan), BF16),
                shape((atoms, chan), BF16),
                shape((POINTS, chan), F32),
            ),
            in_specs=[smem] + [vmem] * 6,
            out_specs=[vmem] * 3,
            scratch_shapes=[
                pltpu.VMEM((atoms, chan), BF16),
                pltpu.VMEM((2 * POINTS, chan), BF16),
                pltpu.VMEM((2 * POINTS, chan), F32),
            ],
            compiler_params=pltpu.CompilerParams(vmem_limit_bytes=16 << 20),
            name="cells",
        )(meta, cs, ct, proj, back, shapes, kf)
        results = pl.pallas_call(
            functools.partial(reduce_kernel, n_dp, n_ka, 1.0 / (2 * chan * chan), 1.0 / (depth * n_ka * chan)),
            out_shape=(
                shape((atoms, chan), BF16), shape((atoms, chan), BF16),
                shape((chan, chan), F32), shape((chan, chan), F32), shape((depth, chan), F32),
            ),
            in_specs=[vmem] * 8,
            out_specs=[vmem] * 5,
            scratch_shapes=[
                pltpu.VMEM((n_dp, height, width), BF16),
                pltpu.VMEM((n_dp - 1, height, width), BF16),
                pltpu.VMEM((n_dp, height, width), BF16),
                pltpu.VMEM((1, depth), F32),
                pltpu.VMEM((n_ka - 1, 1, depth), F32),
                pltpu.VMEM((n_dp, 1, depth), F32),
            ] + [dma((n_dp,))] * 4 + [dma((n_ka,))] * 2 + [dma((n_dp,))] * 2,
            compiler_params=pltpu.CompilerParams(collective_id=1, has_side_effects=True, vmem_limit_bytes=REDUCE_VMEM),
            name="reduce",
        )(act, upd, rsum, feats, cotan, w_in, w_out, kvec)
        return tuple(pl.pallas_call(
            put_kernel,
            out_shape=[shape(r.shape, r.dtype) for r in results],
            in_specs=[vmem] * 5,
            out_specs=[hbm] * 5,
            scratch_shapes=[dma((5,))],
            compiler_params=pltpu.CompilerParams(vmem_limit_bytes=16 << 20),
            name="put",
        )(*results))

    placed = (
        P("dp", None), P(None, "dp"), P("dp", None), P("dp", None, None), P(None, "ka"),
        P(), P(), P("ka", None), P(), P("dp", None),
    )
    return jax.shard_map(
        body,
        mesh=mesh,
        in_specs=placed,
        out_specs=(P("dp", None), P("dp", None), P(), P(), P("ka", None)),
        check_vma=False,
    )
```
